512 devices in a mesh: wave: 4 (over y_hi, core), tx: 8 (over z), ty: 16 (over x, y_lo).
Axes of the slice: x: 4, y: 8 (y_hi: 2, y_lo: 4; y = y_hi * 4 + y_lo), z: 8, core: 2. Of those that a mesh axis runs over, the one named last changes fastest.
Arguments:
- initial_fields: float32 [4, 2, 12, 128, 8192], P('wave', None, None, 'tx', 'ty'), may hold values from -6 to 6
- source_profiles: float32 [4, 2, 3, 8192], P('wave'), may hold values from -6 to 6
- source_waveforms: float32 [4, 2, 5], P('wave'), may hold values from -3 to 3
- material_map: int32 [128, 8192], P('tx', 'ty'), may hold values from 0 to 2
- design_density: float32 [128, 8192], P('tx', 'ty'), may hold values from 0 to 1
- material_table: float32 [3, 4], replicated, may hold values from 0.02 to 12, as said below
- plane_indices: int32 [2], replicated, may hold values from 0 to 127
- design_box: int32 [6], replicated, may hold values from 0 to 128, as said below
Outputs:
- density_gradient: float32 [128, 8192], P('tx', 'ty')
- final_electric: float32 [4, 2, 3, 128, 8192], P('wave', None, None, 'tx', 'ty')
The draws below stay inside these ranges and needn't reach their ends.
Inputs may be any that keep to these rules, and one draw needn't show every extreme that they name: `material_map`: material ids are below 3. `material_table`: column 0 lies in [1, 12], column 1 in [0.5, 3], column 2 in [0.3, 1.5], column 3 in [0.02, 0.5]. `plane_indices`: entry 0 is the source plane of the forward run, entry 1 the monitor plane where the adjoint run's source enters. `design_box`: x0 <= 16, y0 <= 16, x1 = 128, y1 = 128, z0 = 0, z1 = 64.
All inputs are finite; a program needn't handle non-finite values.
Results may differ from the reference program's by a relative error of at most 0.0001.
Values sent between devices are 32-bit elements; how exact they have to be, the bound alone decides.
A program may use at most 64 MiB of HBM per device.

```python
import math
import jax
import jax.numpy as jnp
from jax import lax

NZ = 64
STEPS = 5
NMAT = 3
WAVES = 4
NX = 128
NY = 128


def draw_material_table(key, part):
    keys = jax.random.split(key, 4)
    eps_column = jnp.exp(jax.random.uniform(keys[0], (NMAT,), jnp.float32, 0.0, math.log(12.0)))
    spread_column = jax.random.uniform(keys[1], (NMAT,), jnp.float32, 0.5, 3.0)
    omega_column = jax.random.uniform(keys[2], (NMAT,), jnp.float32, 0.3, 1.5)
    damping_column = jnp.exp(jax.random.uniform(keys[3], (NMAT,), jnp.float32, math.log(0.02), math.log(0.5)))
    return jnp.stack([eps_column, spread_column, omega_column, damping_column], axis=1).astype(jnp.float32)


def draw_design_box(key, part):
    keys = jax.random.split(key, 2)
    rows_low = jax.random.randint(keys[0], (), 0, NX // 8 + 1)
    lines_low = jax.random.randint(keys[1], (), 0, NY // 8 + 1)
    rows_high = jnp.array(NX, jnp.int32)
    lines_high = jnp.array(NY, jnp.int32)
    depth_low = jnp.array(0, jnp.int32)
    depth_high = jnp.array(NZ, jnp.int32)
    return jnp.stack([rows_low, rows_high, lines_low, lines_high, depth_low, depth_high]).astype(jnp.int32)


def plant(values, stream_key, smallest, high):
    place = [jax.random.randint(jax.random.fold_in(stream_key, axis), (), 0, length) for axis, length in enumerate(values.shape)]
    longest = values.shape.index(max(values.shape))
    next_to = place[:longest] + [(place[longest] + 1) % values.shape[longest]] + place[longest + 1:]
    return values.at[tuple(place)].set(smallest).at[tuple(next_to)].set(high)


def block_scale(own_key, extent, shards, smallest, high):
    level, own = 1.0, jax.random.fold_in(own_key, 6)
    for dim, blocks in shards:
        heights = jnp.exp(jax.random.uniform(jax.random.fold_in(own, dim), (blocks,), jnp.float32, smallest / len(shards), high / len(shards)))
        level = level * jnp.repeat(heights, extent[dim] // blocks).reshape([-1 if axis == dim else 1 for axis in range(len(extent))])
    return level


def gaussian(key, dims, deviation, reach, shards=(), held_as=jnp.bfloat16):
    values = deviation * jax.random.normal(key, dims, jnp.float32)
    if shards:
        values = values * block_scale(key, dims, shards, -0.22, 0.18)
    return jnp.clip(values, -reach, reach).astype(held_as)


def setup_inputs(seed: int = 0) -> dict:
    seeds = jax.random.split(jax.random.key(seed), 9)
    initial_fields = gaussian(seeds[0], (WAVES, 2, 12, NX, NY * NZ), 1.0, 6.0, ((0, 4), (3, 8), (4, 16)), jnp.float32)
    source_profiles = gaussian(seeds[1], (WAVES, 2, 3, NY * NZ), 1.0, 6.0, ((0, 4),), jnp.float32)
    source_waveforms = gaussian(seeds[2], (WAVES, 2, STEPS), 1.0, 3.0, ((0, 4),), jnp.float32)
    material_map = plant(jax.random.randint(seeds[3], (NX, NY * NZ), 0, NMAT), jax.random.fold_in(seeds[3], 1), 0, NMAT - 1).astype(jnp.int32)
    design_density = jnp.clip(1.0 * jax.random.uniform(seeds[4], (NX, NY * NZ), jnp.float32) ** block_scale(seeds[4], (NX, NY * NZ), ((0, 8), (1, 16)), -0.2, 0.2), 0.0, 1.0)
    material_table = draw_material_table(jax.random.fold_in(seeds[8], 71), 0)
    plane_indices = jax.random.randint(seeds[6], (2,), 0, NX).astype(jnp.int32)
    design_box = draw_design_box(jax.random.fold_in(seeds[8], 71), 0)
    return {"initial_fields": initial_fields, "source_profiles": source_profiles, "source_waveforms": source_waveforms, "material_map": material_map, "design_density": design_density, "material_table": material_table, "plane_indices": plane_indices, "design_box": design_box}


time_step = 0.5
contrast = 2.0


def ahead_rows(values, border):
    return jnp.concatenate([values[:, 1:], border], axis=1)


def behind_rows(values, border):
    return jnp.concatenate([border, values[:, :-1]], axis=1)


def ahead_lines(values, border):
    width = border.shape[2]
    return jnp.concatenate([values[:, :, width:], border], axis=2)


def behind_lines(values, border):
    width = border.shape[2]
    return jnp.concatenate([border, values[:, :, :-width]], axis=2)


def ahead_depth(values, depth_last):
    shifted = jnp.concatenate([values[:, :, 1:], jnp.zeros_like(values[:, :, :1])], axis=2)
    return jnp.where(depth_last, 0.0, shifted)


def behind_depth(values, depth_first):
    shifted = jnp.concatenate([jnp.zeros_like(values[:, :, :1]), values[:, :, :-1]], axis=2)
    return jnp.where(depth_first, 0.0, shifted)


def curl_electric(field, rows_ahead, lines_ahead, depth_last):
    part_one, part_two, part_three = field[:, 0], field[:, 1], field[:, 2]
    curl_one = (ahead_lines(part_three, lines_ahead[:, 1]) - part_three) - (ahead_depth(part_two, depth_last) - part_two)
    curl_two = (ahead_depth(part_one, depth_last) - part_one) - (ahead_rows(part_three, rows_ahead[:, 1]) - part_three)
    curl_three = (ahead_rows(part_two, rows_ahead[:, 0]) - part_two) - (ahead_lines(part_one, lines_ahead[:, 0]) - part_one)
    return jnp.stack([curl_one, curl_two, curl_three], axis=1)


def curl_magnetic(field, rows_behind, lines_behind, depth_first):
    part_one, part_two, part_three = field[:, 0], field[:, 1], field[:, 2]
    curl_one = (part_three - behind_lines(part_three, lines_behind[:, 1])) - (part_two - behind_depth(part_two, depth_first))
    curl_two = (part_one - behind_depth(part_one, depth_first)) - (part_three - behind_rows(part_three, rows_behind[:, 1]))
    curl_three = (part_two - behind_rows(part_two, rows_behind[:, 0])) - (part_one - behind_lines(part_one, lines_behind[:, 0]))
    return jnp.stack([curl_one, curl_two, curl_three], axis=1)


def zero_borders(field):
    return (jnp.zeros((field.shape[0], 2, 1, field.shape[3]), field.dtype),
            jnp.zeros((field.shape[0], 2, field.shape[2], NZ), field.dtype))


def design_mask(grid_rows, grid_flat, design_box):
    lines = grid_flat // NZ
    depth_ids = grid_flat % NZ
    in_rows = (grid_rows >= design_box[0]) & (grid_rows < design_box[1])
    in_lines = (lines >= design_box[2]) & (lines < design_box[3]) & (depth_ids >= design_box[4]) & (depth_ids < design_box[5])
    return (in_rows[:, None] & in_lines[None, :]).astype(jnp.float32)


def coefficients(material_map, design_density, material_table, inside_design):
    damping = material_table[:, 3]
    denom = 1.0 + 0.25 * damping
    decay = (1.0 - 0.25 * damping) / denom
    drive = material_table[:, 2] * material_table[:, 2] * time_step / denom
    coupled = drive * material_table[:, 1]
    permittivity = jnp.zeros(material_map.shape, jnp.float32)
    decay_map = jnp.zeros(material_map.shape, jnp.float32)
    drive_map = jnp.zeros(material_map.shape, jnp.float32)
    coupled_map = jnp.zeros(material_map.shape, jnp.float32)
    for material_id in range(NMAT):
        chosen = (material_map == material_id).astype(jnp.float32)
        permittivity = permittivity + chosen * material_table[material_id, 0]
        decay_map = decay_map + chosen * decay[material_id]
        drive_map = drive_map + chosen * drive[material_id]
        coupled_map = coupled_map + chosen * coupled[material_id]
    permittivity = permittivity + (inside_design * design_density) * contrast
    return jnp.stack([time_step / permittivity, decay_map, drive_map, coupled_map])


def advance(electric, magnetic, polarization, current, coeffs, inside, depth_last, depth_first, source, electric_borders, magnetic_borders):
    rows_ahead, lines_ahead = electric_borders(electric)
    magnetic = (magnetic - time_step * curl_electric(electric, rows_ahead, lines_ahead, depth_last)) * inside
    current = coeffs[1] * current + coeffs[3] * electric - coeffs[2] * polarization
    polarization = polarization + time_step * current
    rows_behind, lines_behind = magnetic_borders(magnetic)
    electric = electric + coeffs[0] * ((curl_magnetic(magnetic, rows_behind, lines_behind, depth_first) - current) - source)
    return electric, magnetic, polarization, current


def reference(initial_fields, source_profiles, source_waveforms, material_map, design_density, material_table, plane_indices, design_box):
    grid_rows = jnp.arange(NX, dtype=jnp.int32)
    grid_flat = jnp.arange(NY * NZ, dtype=jnp.int32)
    inside_design = design_mask(grid_rows, grid_flat, design_box)
    coeffs = coefficients(material_map, design_density, material_table, inside_design)
    depth_ids = grid_flat % NZ
    depth_last = depth_ids == NZ - 1
    depth_first = depth_ids == 0
    plane_rows = (grid_rows[None, :] == plane_indices[:, None]).astype(jnp.float32)

    def one_channel(inputs):
        fields, profiles, waveforms = inputs
        electric = fields[:, 0:3]
        magnetic = fields[:, 3:6]
        polarization = fields[:, 6:9]
        current = fields[:, 9:12]
        forward_history = [electric[0]]
        adjoint_history = [electric[1]]
        for step_index in range(STEPS):
            source = waveforms[:, step_index][:, None, None, None] * profiles[:, :, None, :] * plane_rows[:, None, :, None]
            electric, magnetic, polarization, current = advance(electric, magnetic, polarization, current, coeffs, 1.0, depth_last, depth_first, source, zero_borders, zero_borders)
            forward_history.append(electric[0])
            adjoint_history.append(electric[1])
        partial_value = jnp.zeros((NX, NY * NZ), jnp.float32)
        for pair_index in range(1, STEPS + 1):
            partial_value = partial_value + jnp.sum(adjoint_history[STEPS + 1 - pair_index] * (forward_history[pair_index] - forward_history[pair_index - 1]), axis=0)
        return electric, partial_value

    finals, partials = lax.map(one_channel, (initial_fields, source_profiles, source_waveforms))
    density_gradient = contrast * inside_design * jnp.sum(partials, axis=0)
    return density_gradient, finals
```

```python
import functools

import jax
import jax.numpy as jnp
from jax import lax
from jax.experimental import pallas as pl
from jax.experimental.pallas import tpu as pltpu
from jax.sharding import PartitionSpec as P

NZ = 64
STEPS = 5
NMAT = 3
LANES = 128
MESH = pl.DeviceIdType.MESH

time_step = 0.5
contrast = 2.0


def kernel(
    sizes,
    fields,
    profiles,
    waveforms,
    material_map,
    density,
    table,
    planes,
    box,
    grad_out,
    final_out,
    state,
    profile,
    source,
    coefs,
    inside,
    moves,
    duals,
    send_xe,
    send_xh,
    send_ye,
    send_yh,
    send_de,
    send_dh,
    recv_xe,
    recv_xh,
    recv_ye,
    recv_yh,
    recv_de,
    recv_dh,
    partial,
    core_in,
    half_sum,
    chip_in,
    total,
    send_sem,
    recv_sem,
    wave_send_sem,
    wave_recv_sem,
    load_sem,
    store_sem,
):
    n_wave, n_tx, n_ty, rows, flat = sizes
    chunks = flat // LANES
    wave = lax.axis_index("wave")
    tx = lax.axis_index("tx")
    ty = lax.axis_index("ty")
    tx_next, tx_prev = lax.rem(tx + 1, n_tx), lax.rem(tx + n_tx - 1, n_tx)
    ty_next, ty_prev = lax.rem(ty + 1, n_ty), lax.rem(ty + n_ty - 1, n_ty)
    core = lax.rem(wave, 2)
    wave_core = wave + 1 - 2 * core
    wave_chip = lax.rem(wave + 2, n_wave)

    load = pltpu.make_async_copy(fields.at[0], state, load_sem.at[0])
    load.start()
    load_profile = pltpu.make_async_copy(
        profiles.at[0, :, :, pl.ds(pl.multiple_of(ty * flat, LANES), flat)], profile, load_sem.at[1]
    )
    load_profile.start()

    barrier = pltpu.get_barrier_semaphore()
    partners = (
        {"tx": tx_prev},
        {"tx": tx_next},
        {"ty": ty_prev},
        {"ty": ty_next},
        {"tx": tx_prev, "ty": ty_next},
        {"tx": tx_next, "ty": ty_prev},
        {"wave": wave_core},
        {"wave": wave_chip},
    )
    for partner in partners:
        pl.semaphore_signal(barrier, inc=1, device_id=partner, device_id_type=MESH)

    row_id = lax.broadcasted_iota(jnp.int32, (rows, LANES), 0)
    lane_id = lax.broadcasted_iota(jnp.int32, (rows, LANES), 1)
    low = lane_id < NZ
    depth = lax.rem(lane_id, NZ)
    depth_first = depth == 0
    depth_last = depth == NZ - 1
    first_row = row_id == 0
    last_row = row_id == rows - 1

    def part(k):
        return slice(k * LANES, (k + 1) * LANES)

    def per_material(material, values):
        out = jnp.where(material == 0, values[0], values[1])
        for m in range(2, NMAT):
            out = jnp.where(material == m, values[m], out)
        return out

    for k in range(chunks):
        material = material_map[:, part(k)]
        eps = per_material(material, [table[m, 0] for m in range(NMAT)])
        spread = per_material(material, [table[m, 1] for m in range(NMAT)])
        omega = per_material(material, [table[m, 2] for m in range(NMAT)])
        damping = per_material(material, [table[m, 3] for m in range(NMAT)])
        x_id = row_id + tx * rows
        y_id = ty * (flat // NZ) + 2 * k + lane_id // NZ
        in_box = (
            (x_id >= box[0])
            & (x_id < box[1])
            & (y_id >= box[2])
            & (y_id < box[3])
            & (depth >= box[4])
            & (depth < box[5])
        )
        within = jnp.where(in_box, 1.0, 0.0)
        inside[:, part(k)] = within
        denom = 1.0 + 0.25 * damping
        drive = omega * omega * time_step / denom
        coefs[0, :, part(k)] = time_step / (eps + (within * density[:, part(k)]) * contrast)
        coefs[1, :, part(k)] = (1.0 - 0.25 * damping) / denom
        coefs[2, :, part(k)] = drive
        coefs[3, :, part(k)] = drive * spread

    load_profile.wait()
    for r in range(2):
        on_plane = jnp.where(row_id + tx * rows == planes[r], 1.0, 0.0)
        for c in range(3):
            for k in range(chunks):
                source[r, c, :, part(k)] = coefs[0, :, part(k)] * on_plane * profile[r, c : c + 1, part(k)]

    keep_x_next = jnp.where(tx == n_tx - 1, 0.0, 1.0)
    keep_x_prev = jnp.where(tx == 0, 0.0, 1.0)
    keep_y_next = jnp.where(ty == n_ty - 1, 0.0, 1.0)
    keep_y_prev = jnp.where(ty == 0, 0.0, 1.0)

    def roll(v, shift, axis):
        return pltpu.roll(v, shift % v.shape[axis], axis)

    def z_up(v):
        return jnp.where(depth_last, 0.0, roll(v, -1, 1))

    def z_down(v):
        return jnp.where(depth_first, 0.0, roll(v, 1, 1))

    def x_up(v):
        return jnp.where(last_row, 0.0, roll(v, -1, 0))

    def x_down(v, ghost):
        return jnp.where(first_row, ghost, roll(v, 1, 0))

    def y_up(vs):
        turned = [roll(v, NZ, 1) for v in vs]
        turned.append(jnp.zeros_like(turned[0]))
        return [jnp.where(low, turned[k], turned[k + 1]) for k in range(chunks)]

    def y_down(vs, ghost):
        turned = [ghost] + [roll(v, NZ, 1) for v in vs]
        return [jnp.where(low, turned[k], turned[k + 1]) for k in range(chunks)]

    def get(r, c):
        return [state[r, c, :, part(k)] for k in range(chunks)]

    def put(r, c, vs):
        for k in range(chunks):
            state[r, c, :, part(k)] = vs[k]

    load.wait()
    pl.semaphore_wait(barrier, len(partners))

    def step(n, carry):
        for r in range(2):
            ex, ey, ez = get(r, 0), get(r, 1), get(r, 2)
            y_ez, y_ex = y_up(ez), y_up(ex)
            for k in range(chunks):
                x_ez, x_ey = x_up(ez[k]), x_up(ey[k])
                z_ey, z_ex = z_up(ey[k]), z_up(ex[k])
                curl_x = (y_ez[k] - ez[k]) - (z_ey - ey[k])
                curl_y = (z_ex - ex[k]) - (x_ez - ez[k])
                curl_z = (x_ey - ey[k]) - (y_ex[k] - ex[k])
                hx = state[r, 3, :, part(k)] - time_step * curl_x
                hy = state[r, 4, :, part(k)] - time_step * curl_y
                hz = state[r, 5, :, part(k)] - time_step * curl_z
                state[r, 3, :, part(k)] = hx
                state[r, 4, :, part(k)] = hy
                state[r, 5, :, part(k)] = hz
                send_xe[n, 2 * r : 2 * r + 1, part(k)] = ey[k][0:1]
                send_xe[n, 2 * r + 1 : 2 * r + 2, part(k)] = ez[k][0:1]
                send_xh[n, 2 * r : 2 * r + 1, part(k)] = hy[rows - 1 : rows]
                send_xh[n, 2 * r + 1 : 2 * r + 2, part(k)] = hz[rows - 1 : rows]
                if k == 0:
                    send_ye[n, r] = jnp.where(low, ex[k], roll(ez[k], NZ, 1))
                    send_dh[n, r : r + 1] = ex[k][rows - 1 : rows]
                if k == chunks - 1:
                    send_yh[n, r] = jnp.where(low, roll(hx, NZ, 1), hz)
                    send_de[n, r : r + 1] = ey[k][0:1]

        copies = []
        flows = (
            (send_ye, recv_ye, {"ty": ty_prev}),
            (send_yh, recv_yh, {"ty": ty_next}),
            (send_de, recv_de, {"tx": tx_prev, "ty": ty_next}),
            (send_dh, recv_dh, {"tx": tx_next, "ty": ty_prev}),
            (send_xe, recv_xe, {"tx": tx_prev}),
            (send_xh, recv_xh, {"tx": tx_next}),
        )
        for i, (src, dst, target) in enumerate(flows):
            copy = pltpu.make_async_remote_copy(
                src_ref=src.at[n],
                dst_ref=dst.at[n],
                send_sem=send_sem.at[n, i],
                recv_sem=recv_sem.at[n, i],
                device_id=target,
                device_id_type=MESH,
            )
            copy.start()
            copies.append(copy)

        for r in range(2):
            for c in range(3):
                for k in range(chunks):
                    e = state[r, c, :, part(k)]
                    p = state[r, 6 + c, :, part(k)]
                    j = state[r, 9 + c, :, part(k)]
                    j = coefs[1, :, part(k)] * j + coefs[3, :, part(k)] * e - coefs[2, :, part(k)] * p
                    state[r, 9 + c, :, part(k)] = j
                    state[r, 6 + c, :, part(k)] = p + time_step * j

        for copy in copies:
            copy.wait_recv()

        for r in range(2):
            ex0, ez0 = state[r, 0, :, part(0)], state[r, 2, :, part(0)]
            got = recv_yh[n, r]
            corner = roll(jnp.broadcast_to(recv_de[n, r : r + 1], (rows, LANES)), NZ, 1) * keep_x_next
            line_hx = (got - time_step * ez0) * keep_y_prev
            line_hz = (
                roll(got, NZ, 1) + time_step * ex0 - jnp.where(last_row, time_step * corner, 0.0)
            ) * keep_y_prev
            row_hy, row_hz = [], []
            for k in range(chunks):
                hy = recv_xh[n, 2 * r : 2 * r + 1, part(k)] + time_step * state[r, 2, 0:1, part(k)]
                hz = recv_xh[n, 2 * r + 1 : 2 * r + 2, part(k)] - time_step * state[r, 1, 0:1, part(k)]
                if k == chunks - 1:
                    edge = roll(recv_dh[n, r : r + 1], NZ, 1) * keep_y_next
                    hz = hz + jnp.where(low[0:1], 0.0, time_step * edge)
                row_hy.append(hy * keep_x_prev)
                row_hz.append(hz * keep_x_prev)

            ahead = recv_ye[n, r] * (time_step * keep_y_next)
            k = chunks - 1
            state[r, 3, :, part(k)] = state[r, 3, :, part(k)] - jnp.where(low, 0.0, ahead)
            state[r, 5, :, part(k)] = state[r, 5, :, part(k)] + jnp.where(low, 0.0, roll(ahead, NZ, 1))
            for k in range(chunks):
                last = slice(rows - 1, rows)
                ey_next = recv_xe[n, 2 * r : 2 * r + 1, part(k)] * (time_step * keep_x_next)
                ez_next = recv_xe[n, 2 * r + 1 : 2 * r + 2, part(k)] * (time_step * keep_x_next)
                state[r, 4, last, part(k)] = state[r, 4, last, part(k)] + ez_next
                state[r, 5, last, part(k)] = state[r, 5, last, part(k)] - ey_next

            hx, hy, hz = get(r, 3), get(r, 4), get(r, 5)
            y_hz, y_hx = y_down(hz, line_hz), y_down(hx, line_hx)
            amount = waveforms[0, r, n]
            for k in range(chunks):
                x_hz, x_hy = x_down(hz[k], row_hz[k]), x_down(hy[k], row_hy[k])
                z_hy, z_hx = z_down(hy[k]), z_down(hx[k])
                curls = (
                    (hz[k] - y_hz[k]) - (hy[k] - z_hy),
                    (hx[k] - z_hx) - (hz[k] - x_hz),
                    (hy[k] - x_hy) - (hx[k] - y_hx[k]),
                )
                for c in range(3):
                    old = state[r, c, :, part(k)]
                    new = (
                        old
                        + coefs[0, :, part(k)] * (curls[c] - state[r, 9 + c, :, part(k)])
                        - amount * source[r, c, :, part(k)]
                    )
                    state[r, c, :, part(k)] = new
                    if r == 0:
                        moves[n, c, :, part(k)] = new - old
                    else:
                        duals[n, c, :, part(k)] = new
        return carry

    lax.fori_loop(0, STEPS, step, 0)

    store = pltpu.make_async_copy(state.at[:, 0:3], final_out.at[0], store_sem.at[0])
    store.start()

    for k in range(chunks):
        value = jnp.zeros((rows, LANES), jnp.float32)
        for n in range(STEPS):
            for c in range(3):
                value = value + duals[STEPS - 1 - n, c, :, part(k)] * moves[n, c, :, part(k)]
        partial[:, part(k)] = value

    half = rows // 2
    mine = pl.ds(pl.multiple_of(core * half, half), half)
    other = pl.ds(pl.multiple_of((1 - core) * half, half), half)

    def wave_copy(i, src, dst, target):
        return pltpu.make_async_remote_copy(
            src_ref=src,
            dst_ref=dst,
            send_sem=wave_send_sem.at[i],
            recv_sem=wave_recv_sem.at[i],
            device_id={"wave": target},
            device_id_type=MESH,
        )

    swap = wave_copy(0, partial.at[other], core_in, wave_core)
    swap.start()
    swap.wait_recv()
    half_sum[...] = partial[mine, :] + core_in[...]
    cross = wave_copy(1, half_sum, chip_in, wave_chip)
    cross.start()
    cross.wait_recv()
    total[mine, :] = (contrast * inside[mine, :]) * (half_sum[...] + chip_in[...])
    back = wave_copy(2, total.at[mine], total.at[mine], wave_core)
    back.start()
    back.wait_recv()
    grad = pltpu.make_async_copy(total, grad_out, store_sem.at[1])
    grad.start()

    swap.wait_send()
    cross.wait_send()
    back.wait_send()

    def drain(n, carry):
        for i, (src, dst, target) in enumerate(
            (
                (send_ye, recv_ye, {"ty": ty_prev}),
                (send_yh, recv_yh, {"ty": ty_next}),
                (send_de, recv_de, {"tx": tx_prev, "ty": ty_next}),
                (send_dh, recv_dh, {"tx": tx_next, "ty": ty_prev}),
                (send_xe, recv_xe, {"tx": tx_prev}),
                (send_xh, recv_xh, {"tx": tx_next}),
            )
        ):
            pltpu.make_async_remote_copy(
                src_ref=src.at[n],
                dst_ref=dst.at[n],
                send_sem=send_sem.at[n, i],
                recv_sem=recv_sem.at[n, i],
                device_id=target,
                device_id_type=MESH,
            ).wait_send()
        return carry

    lax.fori_loop(0, STEPS, drain, 0)
    store.wait()
    grad.wait()


def solution(mesh):
    n_wave, n_tx, n_ty = mesh.shape["wave"], mesh.shape["tx"], mesh.shape["ty"]

    def on_device(fields, profiles, waveforms, material_map, density, table, planes, box):
        rows, flat = material_map.shape
        f32 = jnp.float32
        vmem, smem, anywhere = pltpu.VMEM, pltpu.SMEM, pl.ANY
        spaces = (anywhere, anywhere, smem, vmem, vmem, smem, smem, smem)
        y_halo = (STEPS, 2, rows, LANES)
        x_halo = (STEPS, 4, flat)
        corner = (STEPS, 2, LANES)
        return pl.pallas_call(
            functools.partial(kernel, (n_wave, n_tx, n_ty, rows, flat)),
            out_shape=(
                jax.ShapeDtypeStruct((rows, flat), f32),
                jax.ShapeDtypeStruct((1, 2, 3, rows, flat), f32),
            ),
            in_specs=[pl.BlockSpec(memory_space=space) for space in spaces],
            out_specs=(pl.BlockSpec(memory_space=anywhere),) * 2,
            scratch_shapes=[
                vmem((2, 12, rows, flat), f32),
                vmem((2, 3, flat), f32),
                vmem((2, 3, rows, flat), f32),
                vmem((4, rows, flat), f32),
                vmem((rows, flat), f32),
                vmem((STEPS, 3, rows, flat), f32),
                vmem((STEPS, 3, rows, flat), f32),
                vmem(x_halo, f32),
                vmem(x_halo, f32),
                vmem(y_halo, f32),
                vmem(y_halo, f32),
                vmem(corner, f32),
                vmem(corner, f32),
                vmem(x_halo, f32),
                vmem(x_halo, f32),
                vmem(y_halo, f32),
                vmem(y_halo, f32),
                vmem(corner, f32),
                vmem(corner, f32),
                vmem((rows, flat), f32),
                vmem((rows // 2, flat), f32),
                vmem((rows // 2, flat), f32),
                vmem((rows // 2, flat), f32),
                vmem((rows, flat), f32),
                pltpu.SemaphoreType.DMA((STEPS, 6)),
                pltpu.SemaphoreType.DMA((STEPS, 6)),
                pltpu.SemaphoreType.DMA((3,)),
                pltpu.SemaphoreType.DMA((3,)),
                pltpu.SemaphoreType.DMA((2,)),
                pltpu.SemaphoreType.DMA((2,)),
            ],
            compiler_params=pltpu.CompilerParams(collective_id=0, has_side_effects=True),
        )(fields, profiles, waveforms, material_map, density, table, planes, box)

    placed = (
        P("wave", None, None, "tx", "ty"),
        P("wave", None, None, None),
        P("wave", None, None),
        P("tx", "ty"),
        P("tx", "ty"),
        P(),
        P(),
        P(),
    )
    return jax.shard_map(
        on_device,
        mesh=mesh,
        in_specs=placed,
        out_specs=(P("tx", "ty"), P("wave", None, None, "tx", "ty")),
        check_vma=False,
    )
```

```python
import functools

import jax
import jax.numpy as jnp
from jax import lax
from jax.experimental import pallas as pl
from jax.experimental.pallas import tpu as pltpu
from jax.sharding import PartitionSpec as P

NZ = 64
STEPS = 5
NMAT = 3
LANES = 128
REACH = 4
FLOWS = 16
MESH = pl.DeviceIdType.MESH

time_step = 0.5
contrast = 2.0


def kernel(
    sizes,
    fields,
    profiles,
    waveforms,
    material_map,
    density,
    table,
    planes,
    box,
    grad_out,
    final_out,
    alone,
    wide,
    profile,
    source,
    medium,
    coefs,
    inside,
    moves,
    duals,
    send_y,
    send_x,
    recv_ye,
    recv_yh,
    recv_yc,
    recv_x,
    recv_xc,
    far_x,
    far_y,
    partial,
    core_in,
    half_sum,
    chip_in,
    total,
    send_sem,
    recv_sem,
    once_send_sem,
    once_recv_sem,
    wave_send_sem,
    wave_recv_sem,
    load_sem,
    store_sem,
):
    n_wave, n_tx, n_ty, rows, flat = sizes
    chunks = flat // LANES
    wide_chunks = 2 * chunks
    wide_rows = rows + 2 * REACH
    edge = REACH * NZ
    wave = lax.axis_index("wave")
    tx = lax.axis_index("tx")
    ty = lax.axis_index("ty")
    tx_next, tx_prev = lax.rem(tx + 1, n_tx), lax.rem(tx + n_tx - 1, n_tx)
    ty_next, ty_prev = lax.rem(ty + 1, n_ty), lax.rem(ty + n_ty - 1, n_ty)
    core = lax.rem(wave, 2)
    wave_core = wave + 1 - 2 * core
    wave_chip = lax.rem(wave + 2, n_wave)

    load = pltpu.make_async_copy(fields.at[0], alone, load_sem.at[0])
    load.start()
    load_profile = pltpu.make_async_copy(
        profiles.at[0, :, :, pl.ds(pl.multiple_of(ty * flat, LANES), flat)], profile, load_sem.at[1]
    )
    load_profile.start()
    load_wide = pltpu.make_async_copy(fields.at[0], wide.at[:, :, 0:rows, 0:flat], load_sem.at[2])
    load_wide.start()

    barrier = pltpu.get_barrier_semaphore()
    low_low = {"tx": tx_prev, "ty": ty_prev}
    low_high = {"tx": tx_prev, "ty": ty_next}
    high_low = {"tx": tx_next, "ty": ty_prev}
    high_high = {"tx": tx_next, "ty": ty_next}
    partners = (
        {"ty": ty_prev},
        {"ty": ty_next},
        low_low,
        low_high,
        high_low,
        high_high,
        {"tx": tx_prev},
        {"tx": tx_next},
        {"wave": wave_chip},
        {"wave": wave_core},
    )
    for partner in partners:
        pl.semaphore_signal(barrier, inc=1, device_id=partner, device_id_type=MESH)

    def ids(count):
        row = lax.broadcasted_iota(jnp.int32, (count, LANES), 0)
        lane = lax.broadcasted_iota(jnp.int32, (count, LANES), 1)
        return row, lane, lane < NZ, lax.rem(lane, NZ)

    def part(k):
        return slice(k * LANES, (k + 1) * LANES)

    def per_material(material, values):
        out = jnp.where(material == 0, values[0], values[1])
        for m in range(2, NMAT):
            out = jnp.where(material == m, values[m], out)
        return out

    row_id, lane_id, low, depth = ids(rows)
    for k in range(chunks):
        material = material_map[:, part(k)]
        eps = per_material(material, [table[m, 0] for m in range(NMAT)])
        x_id = row_id + tx * rows
        y_id = ty * (flat // NZ) + 2 * k + lane_id // NZ
        in_box = (
            (x_id >= box[0])
            & (x_id < box[1])
            & (y_id >= box[2])
            & (y_id < box[3])
            & (depth >= box[4])
            & (depth < box[5])
        )
        within = jnp.where(in_box, 1.0, 0.0)
        inside[:, part(k)] = within
        medium[0, 0:rows, part(k)] = time_step / (eps + (within * density[:, part(k)]) * contrast)
        medium[1, 0:rows, part(k)] = material.astype(jnp.float32)

    def coefficients(reach, material):
        omega = per_material(material, [table[m, 2] for m in range(NMAT)])
        spread = per_material(material, [table[m, 1] for m in range(NMAT)])
        damping = per_material(material, [table[m, 3] for m in range(NMAT)])
        denom = 1.0 + 0.25 * damping
        drive = omega * omega * time_step / denom
        return reach, (1.0 - 0.25 * damping) / denom, drive, drive * spread

    for k in range(chunks):
        made = coefficients(medium[0, 0:rows, part(k)], material_map[:, part(k)])
        for i in range(4):
            coefs[i, 0:rows, part(k)] = made[i]

    load_profile.wait()
    for r in range(2):
        on_plane = jnp.where(row_id + tx * rows == planes[r], 1.0, 0.0)
        for c in range(3):
            for k in range(chunks):
                source[r, c, 0:rows, part(k)] = (
                    coefs[0, 0:rows, part(k)] * on_plane * profile[c, r : r + 1, part(k)]
                )
                source[r, c, rows:wide_rows, part(k)] = jnp.zeros((2 * REACH, LANES), jnp.float32)

    keep_x_next = jnp.where(tx == n_tx - 1, 0.0, 1.0)
    keep_x_prev = jnp.where(tx == 0, 0.0, 1.0)
    keep_y_next = jnp.where(ty == n_ty - 1, 0.0, 1.0)
    keep_y_prev = jnp.where(ty == 0, 0.0, 1.0)

    def roll(v, shift, axis):
        return pltpu.roll(v, shift % v.shape[axis], axis)

    def remote(src, dst, sems, target):
        return pltpu.make_async_remote_copy(
            src_ref=src,
            dst_ref=dst,
            send_sem=sems[0],
            recv_sem=sems[1],
            device_id=target,
            device_id_type=MESH,
        )

    top, bottom = slice(0, REACH), slice(rows - REACH, rows)
    after, before = slice(rows, rows + REACH), slice(rows + REACH, wide_rows)
    left, right = slice(0, edge), slice(flat - edge, flat)
    beyond, ahead_of = slice(flat, flat + edge), slice(flat + edge, flat + 2 * edge)
    whole, inner = slice(0, rows), slice(0, flat)

    def medium_copies():
        ways = (
            ({"ty": ty_prev}, whole, left, whole, beyond),
            ({"ty": ty_next}, whole, right, whole, ahead_of),
            (low_low, top, left, after, beyond),
            (low_high, top, right, after, ahead_of),
            (high_low, bottom, left, before, beyond),
            (high_high, bottom, right, before, ahead_of),
            ({"tx": tx_prev}, top, inner, after, inner),
            ({"tx": tx_next}, bottom, inner, before, inner),
        )
        return [
            remote(
                medium.at[:, a, b],
                medium.at[:, c, d],
                (once_send_sem.at[i], once_recv_sem.at[i]),
                target,
            )
            for i, (target, a, b, c, d) in enumerate(ways)
        ]

    def far_copies():
        return [
            remote(
                send_x.at[0, 0:4, LANES : 2 * LANES],
                far_x.at[0:4],
                (once_send_sem.at[8], once_recv_sem.at[8]),
                low_high,
            ),
            remote(
                send_y.at[0, :, rows - 2 * REACH : rows - REACH, 0:LANES],
                far_y.at[:, 0:REACH],
                (once_send_sem.at[9], once_recv_sem.at[9]),
                high_low,
            ),
        ]

    def trace_copies(n):
        e_part, h_part = slice(0, LANES), slice(LANES, 2 * LANES)
        e_rows, h_rows = slice(0, 4), slice(4, 8)
        ways = (
            ({"ty": ty_prev}, send_y.at[n, :, :, e_part], recv_ye.at[n, :, whole]),
            ({"ty": ty_next}, send_y.at[n, :, :, h_part], recv_yh.at[n, :, whole]),
            (low_low, send_y.at[n, :, top, e_part], recv_ye.at[n, :, after]),
            (low_low, send_x.at[n, e_rows, left], recv_x.at[n, e_rows, beyond]),
            (low_high, send_y.at[n, :, top, h_part], recv_yh.at[n, :, after]),
            (low_high, send_x.at[n, e_rows, right], recv_x.at[n, e_rows, ahead_of]),
            (high_low, send_y.at[n, :, bottom, e_part], recv_ye.at[n, :, before]),
            (high_low, send_x.at[n, h_rows, left], recv_x.at[n, h_rows, beyond]),
            (high_high, send_y.at[n, :, bottom, h_part], recv_yh.at[n, :, before]),
            (high_high, send_x.at[n, h_rows, right], recv_x.at[n, h_rows, ahead_of]),
            ({"ty": ty_prev}, send_x.at[n, :, left], recv_xc.at[n, :, 0:edge]),
            ({"ty": ty_next}, send_x.at[n, :, right], recv_xc.at[n, :, edge : 2 * edge]),
            ({"tx": tx_prev}, send_x.at[n, e_rows, :], recv_x.at[n, e_rows, inner]),
            ({"tx": tx_next}, send_x.at[n, h_rows, :], recv_x.at[n, h_rows, inner]),
            ({"tx": tx_prev}, send_y.at[n, :, top, :], recv_yc.at[n, :, 0:REACH]),
            ({"tx": tx_next}, send_y.at[n, :, bottom, :], recv_yc.at[n, :, REACH : 2 * REACH]),
        )
        return [
            remote(src, dst, (send_sem.at[n, i], recv_sem.at[n, i]), target)
            for i, (target, src, dst) in enumerate(ways)
        ]

    load.wait()
    pl.semaphore_wait(barrier, len(partners))
    for copy in medium_copies():
        copy.start()

    def alone_step(n, carry):
        depth_first, depth_last = depth == 0, depth == NZ - 1
        first_row, last_row = row_id == 0, row_id == rows - 1

        def y_up(vs):
            turned = [roll(v, NZ, 1) for v in vs] + [jnp.zeros((rows, LANES), jnp.float32)]
            return [jnp.where(low, turned[k], turned[k + 1]) for k in range(chunks)]

        def y_down(vs):
            turned = [jnp.zeros((rows, LANES), jnp.float32)] + [roll(v, NZ, 1) for v in vs]
            return [jnp.where(low, turned[k], turned[k + 1]) for k in range(chunks)]

        def get(r, c):
            return [alone[r, c, :, part(k)] for k in range(chunks)]

        for r in range(2):
            ex, ey, ez = get(r, 0), get(r, 1), get(r, 2)
            y_ez, y_ex = y_up(ez), y_up(ex)
            for k in range(chunks):
                x_ez = jnp.where(last_row, 0.0, roll(ez[k], -1, 0))
                x_ey = jnp.where(last_row, 0.0, roll(ey[k], -1, 0))
                z_ey = jnp.where(depth_last, 0.0, roll(ey[k], -1, 1))
                z_ex = jnp.where(depth_last, 0.0, roll(ex[k], -1, 1))
                curl_x = (y_ez[k] - ez[k]) - (z_ey - ey[k])
                curl_y = (z_ex - ex[k]) - (x_ez - ez[k])
                curl_z = (x_ey - ey[k]) - (y_ex[k] - ex[k])
                hx = alone[r, 3, :, part(k)] - time_step * curl_x
                hy = alone[r, 4, :, part(k)] - time_step * curl_y
                hz = alone[r, 5, :, part(k)] - time_step * curl_z
                alone[r, 3, :, part(k)] = hx
                alone[r, 4, :, part(k)] = hy
                alone[r, 5, :, part(k)] = hz
                send_x[n, 2 * r : 2 * r + 1, part(k)] = ey[k][0:1]
                send_x[n, 2 * r + 1 : 2 * r + 2, part(k)] = ez[k][0:1]
                send_x[n, 4 + 2 * r : 5 + 2 * r, part(k)] = hy[rows - 1 : rows]
                send_x[n, 5 + 2 * r : 6 + 2 * r, part(k)] = hz[rows - 1 : rows]
                if k == 0:
                    send_y[n, r, :, 0:LANES] = jnp.where(low, ex[k], roll(ez[k], NZ, 1))
                if k == chunks - 1:
                    send_y[n, r, :, LANES : 2 * LANES] = jnp.where(low, roll(hx, NZ, 1), hz)

        for copy in trace_copies(n):
            copy.start()

        @pl.when(n == 0)
        def _():
            for copy in far_copies():
                copy.start()

        @pl.when(n < STEPS - 1)
        def _():
            for r in range(2):
                hx, hy, hz = get(r, 3), get(r, 4), get(r, 5)
                y_hz, y_hx = y_down(hz), y_down(hx)
                amount = waveforms[0, r, n]
                for k in range(chunks):
                    x_hz = jnp.where(first_row, 0.0, roll(hz[k], 1, 0))
                    x_hy = jnp.where(first_row, 0.0, roll(hy[k], 1, 0))
                    z_hy = jnp.where(depth_first, 0.0, roll(hy[k], 1, 1))
                    z_hx = jnp.where(depth_first, 0.0, roll(hx[k], 1, 1))
                    curls = (
                        (hz[k] - y_hz[k]) - (hy[k] - z_hy),
                        (hx[k] - z_hx) - (hz[k] - x_hz),
                        (hy[k] - x_hy) - (hx[k] - y_hx[k]),
                    )
                    for c in range(3):
                        e = alone[r, c, :, part(k)]
                        p = alone[r, 6 + c, :, part(k)]
                        j = alone[r, 9 + c, :, part(k)]
                        j = (
                            coefs[1, 0:rows, part(k)] * j
                            + coefs[3, 0:rows, part(k)] * e
                            - coefs[2, 0:rows, part(k)] * p
                        )
                        alone[r, 9 + c, :, part(k)] = j
                        alone[r, 6 + c, :, part(k)] = p + time_step * j
                        alone[r, c, :, part(k)] = (
                            e
                            + coefs[0, 0:rows, part(k)] * (curls[c] - j)
                            - amount * source[r, c, 0:rows, part(k)]
                        )

        return carry

    lax.fori_loop(0, STEPS, alone_step, 0)

    load_wide.wait()
    for r in range(2):
        for c in range(12):
            for k in range(wide_chunks):
                if k < chunks:
                    wide[r, c, rows:wide_rows, part(k)] = jnp.zeros((2 * REACH, LANES), jnp.float32)
                else:
                    wide[r, c, :, part(k)] = jnp.zeros((wide_rows, LANES), jnp.float32)

    for copy in medium_copies():
        copy.wait_recv()
    row_id, lane_id, low, depth = ids(wide_rows)
    near_row = jnp.where(row_id < rows + REACH, row_id, row_id - wide_rows)
    x_in = (near_row + tx * rows >= 0) & (near_row + tx * rows < n_tx * rows)
    for k in range(wide_chunks):
        line = 2 * k if k < chunks + chunks // 2 else 2 * (k - wide_chunks)
        y_id = ty * (flat // NZ) + line + lane_id // NZ
        present = x_in & (y_id >= 0) & (y_id < n_ty * (flat // NZ))
        made = coefficients(medium[0, :, part(k)], medium[1, :, part(k)])
        coefs[0, :, part(k)] = jnp.where(present, made[0], 0.0)
        for i in range(1, 4):
            coefs[i, :, part(k)] = made[i]
        coefs[4, :, part(k)] = jnp.where(present, time_step, 0.0)

    for copy in far_copies():
        copy.wait_recv()

    def wide_step(n, carry):
        depth_first, depth_last = depth == 0, depth == NZ - 1
        start = jnp.where(n == 0, 1.0, 0.0)
        for copy in trace_copies(n):
            copy.wait_recv()

        def get(r, c):
            return [wide[r, c, :, part(k)] for k in range(wide_chunks)]

        def tall(v):
            return jnp.concatenate([jnp.zeros((rows, LANES), jnp.float32), v], axis=0)

        def at_row(i, v):
            return jnp.where(row_id == i, v, 0.0)

        def y_up(vs, inner_edge, outer_edge):
            turned = [roll(v, NZ, 1) for v in vs]
            out = []
            for k in range(wide_chunks):
                other = turned[(k + 1) % wide_chunks]
                if k == chunks - 1:
                    other = other + inner_edge
                if k == chunks + chunks // 2 - 1:
                    other = jnp.zeros_like(other)
                if k == wide_chunks - 1:
                    other = other + outer_edge
                out.append(jnp.where(low, turned[k], other))
            return out

        def y_down(vs, inner_edge, outer_edge, far):
            turned = [roll(v, NZ, 1) for v in vs]
            out = []
            for k in range(wide_chunks):
                other = turned[(k - 1) % wide_chunks]
                if k == 0:
                    other = other + inner_edge
                if k == chunks:
                    other = other + outer_edge
                if k == chunks + chunks // 2:
                    other = far
                out.append(jnp.where(low, other, turned[k]))
            return out

        zero = jnp.zeros((wide_rows, LANES), jnp.float32)
        for r in range(2):
            def x_up(v, k, c):
                out = roll(v, -1, 0) + at_row(rows - 1, keep_x_next * recv_x[n, 2 * r + c : 2 * r + c + 1, part(k)])
                if k >= chunks:
                    out = out + at_row(wide_rows - 1, recv_xc[n, 2 * r + c : 2 * r + c + 1, part(k - chunks)])
                return out

            def x_down(v, k, c, far):
                i = 4 + 2 * r + c
                out = jnp.where(row_id == rows + REACH, far, roll(v, 1, 0))
                out = out + at_row(0, keep_x_prev * recv_x[n, i : i + 1, part(k)])
                if k >= chunks:
                    out = out + at_row(rows, recv_xc[n, i : i + 1, part(k - chunks)])
                return out

            ex, ey, ez = get(r, 0), get(r, 1), get(r, 2)
            got = recv_ye[n, r] * keep_y_next
            corner = tall(recv_yc[n, r, :, 0:LANES])
            y_ez = y_up(ez, got, corner)
            y_ex = y_up(ex, roll(got, NZ, 1), roll(corner, NZ, 1))
            for k in range(wide_chunks):
                x_ez, x_ey = x_up(ez[k], k, 1), x_up(ey[k], k, 0)
                z_ey = jnp.where(depth_last, 0.0, roll(ey[k], -1, 1))
                z_ex = jnp.where(depth_last, 0.0, roll(ex[k], -1, 1))
                curls = (
                    (y_ez[k] - ez[k]) - (z_ey - ey[k]),
                    (z_ex - ex[k]) - (x_ez - ez[k]),
                    (x_ey - ey[k]) - (y_ex[k] - ex[k]),
                )
                for c in range(3):
                    wide[r, 3 + c, :, part(k)] = wide[r, 3 + c, :, part(k)] - coefs[4, :, part(k)] * curls[c]

            hx, hy, hz = get(r, 3), get(r, 4), get(r, 5)
            got = recv_yh[n, r] * keep_y_prev
            corner = tall(recv_yc[n, r, :, LANES : 2 * LANES])
            far_line = at_row(
                rows - 1, (-time_step * start * keep_x_next) * roll(far_x[2 * r : 2 * r + 1], NZ, 1)
            )
            far_row = jnp.where(
                low[0:1], 0.0, (time_step * start * keep_y_next) * roll(far_y[r, REACH - 1 : REACH], NZ, 1)
            )
            y_hx = y_down(hx, got, corner, zero)
            y_hz = y_down(hz, roll(got, NZ, 1), roll(corner, NZ, 1), far_line)
            amount = waveforms[0, r, n]
            for k in range(wide_chunks):
                x_hz = x_down(hz[k], k, 1, far_row if k == chunks - 1 else 0.0)
                x_hy = x_down(hy[k], k, 0, 0.0)
                z_hy = jnp.where(depth_first, 0.0, roll(hy[k], 1, 1))
                z_hx = jnp.where(depth_first, 0.0, roll(hx[k], 1, 1))
                curls = (
                    (hz[k] - y_hz[k]) - (hy[k] - z_hy),
                    (hx[k] - z_hx) - (hz[k] - x_hz),
                    (hy[k] - x_hy) - (hx[k] - y_hx[k]),
                )
                for c in range(3):
                    e = wide[r, c, :, part(k)]
                    p = wide[r, 6 + c, :, part(k)]
                    j = wide[r, 9 + c, :, part(k)]
                    j = coefs[1, :, part(k)] * j + coefs[3, :, part(k)] * e - coefs[2, :, part(k)] * p
                    wide[r, 9 + c, :, part(k)] = j
                    wide[r, 6 + c, :, part(k)] = p + time_step * j
                    new = e + coefs[0, :, part(k)] * (curls[c] - j)
                    if k < chunks:
                        new = new - amount * source[r, c, :, part(k)]
                        if r == 0:
                            moves[n, c, :, part(k)] = new[0:rows] - e[0:rows]
                        else:
                            duals[n, c, :, part(k)] = new[0:rows]
                    wide[r, c, :, part(k)] = new
        return carry

    lax.fori_loop(0, STEPS, wide_step, 0)

    store = pltpu.make_async_copy(wide.at[:, 0:3, 0:rows, 0:flat], final_out.at[0], store_sem.at[0])
    store.start()

    for k in range(chunks):
        value = jnp.zeros((rows, LANES), jnp.float32)
        for n in range(STEPS):
            for c in range(3):
                value = value + duals[STEPS - 1 - n, c, :, part(k)] * moves[n, c, :, part(k)]
        partial[:, part(k)] = value

    half = rows // 2
    mine = pl.ds(pl.multiple_of(core * half, half), half)
    other = pl.ds(pl.multiple_of((1 - core) * half, half), half)

    def wave_copy(i, src, dst, target):
        return pltpu.make_async_remote_copy(
            src_ref=src,
            dst_ref=dst,
            send_sem=wave_send_sem.at[i],
            recv_sem=wave_recv_sem.at[i],
            device_id={"wave": target},
            device_id_type=MESH,
        )

    swap = wave_copy(0, partial.at[other], core_in, wave_core)
    swap.start()
    swap.wait_recv()
    half_sum[...] = partial[mine, :] + core_in[...]
    cross = wave_copy(1, half_sum, chip_in, wave_chip)
    cross.start()
    cross.wait_recv()
    total[mine, :] = (contrast * inside[mine, :]) * (half_sum[...] + chip_in[...])
    back = wave_copy(2, total.at[mine], total.at[mine], wave_core)
    back.start()
    back.wait_recv()
    grad = pltpu.make_async_copy(total, grad_out, store_sem.at[1])
    grad.start()

    swap.wait_send()
    cross.wait_send()
    back.wait_send()

    for copy in medium_copies() + far_copies():
        copy.wait_send()

    def drain(n, carry):
        for copy in trace_copies(n):
            copy.wait_send()
        return carry

    lax.fori_loop(0, STEPS, drain, 0)
    store.wait()
    grad.wait()


def solution(mesh):
    n_wave, n_tx, n_ty = mesh.shape["wave"], mesh.shape["tx"], mesh.shape["ty"]

    def on_device(fields, profiles, waveforms, material_map, density, table, planes, box):
        rows, flat = material_map.shape
        f32 = jnp.float32
        vmem, smem, anywhere = pltpu.VMEM, pltpu.SMEM, pl.ANY
        spaces = (anywhere, anywhere, smem, vmem, vmem, smem, smem, smem)
        wide_rows, wide_flat = rows + 2 * REACH, flat + 2 * REACH * NZ
        return pl.pallas_call(
            functools.partial(kernel, (n_wave, n_tx, n_ty, rows, flat)),
            out_shape=(
                jax.ShapeDtypeStruct((rows, flat), f32),
                jax.ShapeDtypeStruct((1, 2, 3, rows, flat), f32),
            ),
            in_specs=[pl.BlockSpec(memory_space=space) for space in spaces],
            out_specs=(pl.BlockSpec(memory_space=anywhere),) * 2,
            scratch_shapes=[
                vmem((2, 12, rows, flat), f32),
                vmem((2, 12, wide_rows, wide_flat), f32),
                vmem((3, 2, flat), f32),
                vmem((2, 3, wide_rows, flat), f32),
                vmem((2, wide_rows, wide_flat), f32),
                vmem((5, wide_rows, wide_flat), f32),
                vmem((rows, flat), f32),
                vmem((STEPS, 3, rows, flat), f32),
                vmem((STEPS, 3, rows, flat), f32),
                vmem((STEPS, 2, rows, 2 * LANES), f32),
                vmem((STEPS, 8, flat), f32),
                vmem((STEPS, 2, wide_rows, LANES), f32),
                vmem((STEPS, 2, wide_rows, LANES), f32),
                vmem((STEPS, 2, 2 * REACH, 2 * LANES), f32),
                vmem((STEPS, 8, wide_flat), f32),
                vmem((STEPS, 8, 2 * REACH * NZ), f32),
                vmem((8, LANES), f32),
                vmem((2, 8, LANES), f32),
                vmem((rows, flat), f32),
                vmem((rows // 2, flat), f32),
                vmem((rows // 2, flat), f32),
                vmem((rows // 2, flat), f32),
                vmem((rows, flat), f32),
                pltpu.SemaphoreType.DMA((STEPS, FLOWS)),
                pltpu.SemaphoreType.DMA((STEPS, FLOWS)),
                pltpu.SemaphoreType.DMA((10,)),
                pltpu.SemaphoreType.DMA((10,)),
                pltpu.SemaphoreType.DMA((3,)),
                pltpu.SemaphoreType.DMA((3,)),
                pltpu.SemaphoreType.DMA((3,)),
                pltpu.SemaphoreType.DMA((2,)),
            ],
            compiler_params=pltpu.CompilerParams(collective_id=0, has_side_effects=True),
        )(fields, jnp.transpose(profiles, (0, 2, 1, 3)), waveforms, material_map, density, table, planes, box)

    placed = (
        P("wave", None, None, "tx", "ty"),
        P("wave", None, None, None),
        P("wave", None, None),
        P("tx", "ty"),
        P("tx", "ty"),
        P(),
        P(),
        P(),
    )
    return jax.shard_map(
        on_device,
        mesh=mesh,
        in_specs=placed,
        out_specs=(P("tx", "ty"), P("wave", None, None, "tx", "ty")),
        check_vma=False,
    )
```

```python
import functools

import jax
import jax.numpy as jnp
from jax import lax
from jax.experimental import pallas as pl
from jax.experimental.pallas import tpu as pltpu
from jax.sharding import PartitionSpec as P

NZ = 64
STEPS = 5
NMAT = 3
LANES = 128
REACH = 4
FLOWS = 8
MESH = pl.DeviceIdType.MESH

time_step = 0.5
contrast = 2.0


def kernel(
    sizes,
    fields,
    profiles,
    waveforms_in,
    material_in,
    density_in,
    table_in,
    planes_in,
    box_in,
    grad_out,
    final_out,
    alone,
    wide,
    profile,
    source,
    medium,
    coefs,
    inside,
    moves,
    duals,
    send_a,
    send_b,
    send_c,
    send_d,
    recv_a,
    recv_b,
    recv_c,
    recv_d,
    recv_ahead_up,
    recv_ahead_down,
    recv_back_up,
    recv_back_down,
    waveforms,
    material_map,
    density,
    table,
    planes,
    box,
    partial,
    core_in,
    half_sum,
    chip_in,
    send_sem,
    recv_sem,
    once_send_sem,
    once_recv_sem,
    wave_send_sem,
    wave_recv_sem,
    load_sem,
    store_sem,
):
    n_wave, n_tx, n_ty, rows, flat = sizes
    chunks = flat // LANES
    wide_chunks = 2 * chunks
    wide_rows = rows + 2 * REACH
    edge = REACH * NZ
    wave = lax.axis_index("wave")
    tx = lax.axis_index("tx")
    ty = lax.axis_index("ty")
    tx_next, tx_prev = lax.rem(tx + 1, n_tx), lax.rem(tx + n_tx - 1, n_tx)
    ty_next, ty_prev = lax.rem(ty + 1, n_ty), lax.rem(ty + n_ty - 1, n_ty)
    core = lax.rem(wave, 2)
    wave_core = wave + 1 - 2 * core
    wave_chip = lax.rem(wave + 2, n_wave)

    load = pltpu.make_async_copy(fields.at[0, :, 0:6], alone.at[:, 0:6], load_sem.at[0])
    load.start()
    load_rest = pltpu.make_async_copy(fields.at[0, :, 6:12], alone.at[:, 6:12], load_sem.at[3])
    load_rest.start()
    load_profile = pltpu.make_async_copy(
        profiles.at[0, :, :, pl.ds(pl.multiple_of(ty * flat, LANES), flat)], profile, load_sem.at[1]
    )
    load_profile.start()
    small = [
        pltpu.make_async_copy(src, dst, load_sem.at[4 + i])
        for i, (src, dst) in enumerate(
            (
                (material_in, material_map),
                (density_in, density),
                (table_in, table),
                (box_in, box),
                (planes_in, planes),
                (waveforms_in, waveforms),
            )
        )
    ]
    for copy in small:
        copy.start()
    load_wide = pltpu.make_async_copy(fields.at[0], wide.at[:, :, 0:rows, 0:flat], load_sem.at[2])
    load_wide.start()

    barrier = pltpu.get_barrier_semaphore()
    low_low = {"tx": tx_prev, "ty": ty_prev}
    low_high = {"tx": tx_prev, "ty": ty_next}
    high_low = {"tx": tx_next, "ty": ty_prev}
    high_high = {"tx": tx_next, "ty": ty_next}
    partners = (
        {"ty": ty_prev},
        {"ty": ty_next},
        low_low,
        low_high,
        high_low,
        high_high,
        {"tx": tx_prev},
        {"tx": tx_next},
        {"wave": wave_chip},
        {"wave": wave_core},
    )
    for partner in partners:
        pl.semaphore_signal(barrier, inc=1, device_id=partner, device_id_type=MESH)

    def ids(count):
        row = lax.broadcasted_iota(jnp.int32, (count, LANES), 0)
        lane = lax.broadcasted_iota(jnp.int32, (count, LANES), 1)
        return row, lane, lane < NZ, lax.rem(lane, NZ)

    def part(k):
        return slice(k * LANES, (k + 1) * LANES)

    def per_material(material, values):
        out = jnp.where(material == 0, values[0], values[1])
        for m in range(2, NMAT):
            out = jnp.where(material == m, values[m], out)
        return out

    row_id, lane_id, low, depth = ids(rows)

    def coefficients(reach, material):
        omega = per_material(material, [table[m, 2] for m in range(NMAT)])
        spread = per_material(material, [table[m, 1] for m in range(NMAT)])
        damping = per_material(material, [table[m, 3] for m in range(NMAT)])
        denom = 1.0 + 0.25 * damping
        drive = omega * omega * time_step / denom
        return reach, (1.0 - 0.25 * damping) / denom, drive, drive * spread

    def prepare():
        for copy in small:
            copy.wait()
        load_rest.wait()
        load_profile.wait()
        for k in range(chunks):
            material = material_map[:, part(k)]
            eps = per_material(material, [table[m, 0] for m in range(NMAT)])
            x_id = row_id + tx * rows
            y_id = ty * (flat // NZ) + 2 * k + lane_id // NZ
            in_box = (
                (x_id >= box[0])
                & (x_id < box[1])
                & (y_id >= box[2])
                & (y_id < box[3])
                & (depth >= box[4])
                & (depth < box[5])
            )
            within = jnp.where(in_box, 1.0, 0.0)
            inside[:, part(k)] = within
            medium[0, 0:rows, part(k)] = time_step / (eps + (within * density[:, part(k)]) * contrast)
            medium[1, 0:rows, part(k)] = material.astype(jnp.float32)
        for k in range(chunks):
            made = coefficients(medium[0, 0:rows, part(k)], material_map[:, part(k)])
            for i in range(4):
                coefs[i, 0:rows, part(k)] = made[i]

        for r in range(2):
            on_plane = jnp.where(row_id + tx * rows == planes[r], 1.0, 0.0)
            for c in range(3):
                for k in range(chunks):
                    source[r, c, 0:rows, part(k)] = (
                        coefs[0, 0:rows, part(k)] * on_plane * profile[c, r : r + 1, part(k)]
                    )
                    source[r, c, rows:wide_rows, part(k)] = jnp.zeros((2 * REACH, LANES), jnp.float32)

    keep_x_next = jnp.where(tx == n_tx - 1, 0.0, 1.0)
    keep_x_prev = jnp.where(tx == 0, 0.0, 1.0)
    keep_y_next = jnp.where(ty == n_ty - 1, 0.0, 1.0)
    keep_y_prev = jnp.where(ty == 0, 0.0, 1.0)

    def roll(v, shift, axis):
        return pltpu.roll(v, shift % v.shape[axis], axis)

    def remote(src, dst, sems, target):
        return pltpu.make_async_remote_copy(
            src_ref=src,
            dst_ref=dst,
            send_sem=sems[0],
            recv_sem=sems[1],
            device_id=target,
            device_id_type=MESH,
        )

    top, bottom = slice(0, REACH), slice(rows - REACH, rows)
    after, before = slice(rows, rows + REACH), slice(rows + REACH, wide_rows)
    left, right = slice(0, edge), slice(flat - edge, flat)
    beyond, ahead_of = slice(flat, flat + edge), slice(flat + edge, flat + 2 * edge)
    whole, inner = slice(0, rows), slice(0, flat)

    def medium_copies():
        ways = (
            ({"ty": ty_prev}, whole, left, whole, beyond),
            ({"ty": ty_next}, whole, right, whole, ahead_of),
            (low_low, top, left, after, beyond),
            (low_high, top, right, after, ahead_of),
            (high_low, bottom, left, before, beyond),
            (high_high, bottom, right, before, ahead_of),
            ({"tx": tx_prev}, top, inner, after, inner),
            ({"tx": tx_next}, bottom, inner, before, inner),
        )
        return [
            remote(
                medium.at[core, a, b],
                medium.at[core, c, d],
                (once_send_sem.at[i], once_recv_sem.at[i]),
                target,
            )
            for i, (target, a, b, c, d) in enumerate(ways)
        ]

    def shared_copies(plane):
        areas = ((slice(0, rows), slice(flat, 2 * flat)), (slice(rows, wide_rows), slice(0, 2 * flat)))
        return [
            remote(
                medium.at[plane, a, b],
                medium.at[plane, a, b],
                (once_send_sem.at[8 + i], once_recv_sem.at[8 + i]),
                {"wave": wave_core},
            )
            for i, (a, b) in enumerate(areas)
        ]

    def trace_copies(n):
        always, first, later = None, n == 0, n > 0
        early, late, before_last = n < 2, n >= 2, n < STEPS - 1
        ways = (
            (early, 0, {"ty": ty_prev}, send_c.at[n, 0:6], recv_c.at[n, 0:6]),
            (late, 0, {"ty": ty_prev}, send_c.at[n, 0:5], recv_c.at[n, 0:5]),
            (early, 1, {"ty": ty_next}, send_d.at[n, 0:6], recv_d.at[n, 0:6]),
            (late, 1, {"ty": ty_next}, send_d.at[n, 0:5], recv_d.at[n, 0:5]),
            (first, 2, low_high, send_a.at[n], recv_back_up.at[n]),
            (later, 2, low_high, send_a.at[n, 2:4], recv_back_up.at[n, 2:4]),
            (first, 3, high_low, send_b.at[n, 0:3], recv_ahead_down.at[n]),
            (later, 3, high_low, send_b.at[n, 1:3], recv_ahead_down.at[n, 1:3]),
            (before_last, 4, low_low, send_a.at[n, 0:2], recv_ahead_up.at[n]),
            (before_last, 5, high_high, send_b.at[n, 3:5], recv_back_down.at[n]),
            (always, 6, {"tx": tx_prev}, send_a.at[n], recv_a.at[n]),
            (always, 7, {"tx": tx_next}, send_b.at[n, 1:5], recv_b.at[n]),
        )
        return [
            (when, remote(src, dst, (send_sem.at[n, i], recv_sem.at[n, i]), target))
            for when, i, target, src, dst in ways
        ]

    def each_trace(n, act):
        for when, copy in trace_copies(n):
            if when is None:
                act(copy)
            else:

                @pl.when(when)
                def _(copy=copy):
                    act(copy)

    def clear(ref):
        ref[...] = jnp.zeros(ref.shape, jnp.float32)

    clear(recv_c.at[2:STEPS, 5])
    clear(recv_d.at[2:STEPS, 5])
    clear(recv_ahead_up.at[STEPS - 1])
    clear(recv_back_down.at[STEPS - 1])

    load.wait()
    pl.semaphore_wait(barrier, len(partners))

    def alone_step(n, carry):
        depth_first, depth_last = depth == 0, depth == NZ - 1
        first_row, last_row = row_id == 0, row_id == rows - 1

        def y_up(vs):
            turned = [roll(v, NZ, 1) for v in vs] + [jnp.zeros((rows, LANES), jnp.float32)]
            return [jnp.where(low, turned[k], turned[k + 1]) for k in range(chunks)]

        def y_down(vs):
            turned = [jnp.zeros((rows, LANES), jnp.float32)] + [roll(v, NZ, 1) for v in vs]
            return [jnp.where(low, turned[k], turned[k + 1]) for k in range(chunks)]

        def get(r, c):
            return [alone[r, c, :, part(k)] for k in range(chunks)]

        for r in range(2):
            ex, ey, ez = get(r, 0), get(r, 1), get(r, 2)
            y_ez, y_ex = y_up(ez), y_up(ex)
            for k in range(chunks):
                x_ez = jnp.where(last_row, 0.0, roll(ez[k], -1, 0))
                x_ey = jnp.where(last_row, 0.0, roll(ey[k], -1, 0))
                z_ey = jnp.where(depth_last, 0.0, roll(ey[k], -1, 1))
                z_ex = jnp.where(depth_last, 0.0, roll(ex[k], -1, 1))
                curl_x = (y_ez[k] - ez[k]) - (z_ey - ey[k])
                curl_y = (z_ex - ex[k]) - (x_ez - ez[k])
                curl_z = (x_ey - ey[k]) - (y_ex[k] - ex[k])
                hx = alone[r, 3, :, part(k)] - time_step * curl_x
                hy = alone[r, 4, :, part(k)] - time_step * curl_y
                hz = alone[r, 5, :, part(k)] - time_step * curl_z
                alone[r, 3, :, part(k)] = hx
                alone[r, 4, :, part(k)] = hy
                alone[r, 5, :, part(k)] = hz
                e_edge = (ey[k][0:1], ez[k][0:1])
                h_edge = (hy[rows - 1 : rows], hz[rows - 1 : rows])
                side, tile, beside = (
                    (send_c, 4 + k, 0) if k < chunks // 2 else (send_d, 3 + chunks - k, 3)
                )
                for c in range(2):
                    i, j = 4 * (k % 2) + 2 * r + c, 2 * r + c
                    send_a[n, beside, i : i + 1] = e_edge[c]
                    send_b[n, beside + 1, i : i + 1] = h_edge[c]
                    side[n, tile, j : j + 1] = e_edge[c]
                    side[n, tile, 4 + j : 5 + j] = h_edge[c]
                spot = slice(4 * r, 4 * r + 4)
                if k == 0:
                    line = jnp.where(low, ex[k], roll(ez[k], NZ, 1))
                    upper, lower = line[0:8], line[8:16]
                    send_c[n, 2 * r], send_c[n, 2 * r + 1] = upper, lower
                    send_a[n, 1, spot] = (upper if r == 0 else roll(upper, 4, 0))[spot]
                    send_b[n, 2, spot] = (roll(lower, 4, 0) if r == 0 else lower)[spot]
                    send_b[n, 0, spot] = (lower if r == 0 else roll(lower, 4, 0))[spot]
                if k == chunks - 1:
                    line = jnp.where(low, roll(hx, NZ, 1), hz)
                    upper, lower = line[0:8], line[8:16]
                    send_d[n, 2 * r], send_d[n, 2 * r + 1] = upper, lower
                    send_a[n, 2, spot] = (upper if r == 0 else roll(upper, 4, 0))[spot]
                    send_b[n, 3, spot] = (roll(lower, 4, 0) if r == 0 else lower)[spot]

        each_trace(n, lambda copy: copy.start())

        @pl.when(n == 0)
        def _():
            prepare()
            for copy in medium_copies():
                copy.start()

        @pl.when(n < STEPS - 1)
        def _():
            for r in range(2):
                hx, hy, hz = get(r, 3), get(r, 4), get(r, 5)
                y_hz, y_hx = y_down(hz), y_down(hx)
                amount = waveforms[0, r, n]
                for k in range(chunks):
                    x_hz = jnp.where(first_row, 0.0, roll(hz[k], 1, 0))
                    x_hy = jnp.where(first_row, 0.0, roll(hy[k], 1, 0))
                    z_hy = jnp.where(depth_first, 0.0, roll(hy[k], 1, 1))
                    z_hx = jnp.where(depth_first, 0.0, roll(hx[k], 1, 1))
                    curls = (
                        (hz[k] - y_hz[k]) - (hy[k] - z_hy),
                        (hx[k] - z_hx) - (hz[k] - x_hz),
                        (hy[k] - x_hy) - (hx[k] - y_hx[k]),
                    )
                    for c in range(3):
                        e = alone[r, c, :, part(k)]
                        p = alone[r, 6 + c, :, part(k)]
                        j = alone[r, 9 + c, :, part(k)]
                        j = (
                            coefs[1, 0:rows, part(k)] * j
                            + coefs[3, 0:rows, part(k)] * e
                            - coefs[2, 0:rows, part(k)] * p
                        )
                        alone[r, 9 + c, :, part(k)] = j
                        alone[r, 6 + c, :, part(k)] = p + time_step * j
                        alone[r, c, :, part(k)] = (
                            e
                            + coefs[0, 0:rows, part(k)] * (curls[c] - j)
                            - amount * source[r, c, 0:rows, part(k)]
                        )

        return carry

    lax.fori_loop(0, STEPS, alone_step, 0)

    for copy in medium_copies():
        copy.wait_recv()
    for copy in shared_copies(core):
        copy.start()

    load_wide.wait()
    for r in range(2):
        for c in range(12):
            for k in range(wide_chunks):
                if k < chunks:
                    wide[r, c, rows:wide_rows, part(k)] = jnp.zeros((2 * REACH, LANES), jnp.float32)
                else:
                    wide[r, c, :, part(k)] = jnp.zeros((wide_rows, LANES), jnp.float32)

    for copy in shared_copies(1 - core):
        copy.wait_recv()
    row_id, lane_id, low, depth = ids(wide_rows)
    near_row = jnp.where(row_id < rows + REACH, row_id, row_id - wide_rows)
    x_in = (near_row + tx * rows >= 0) & (near_row + tx * rows < n_tx * rows)
    for k in range(wide_chunks):
        line = 2 * k if k < chunks + chunks // 2 else 2 * (k - wide_chunks)
        y_id = ty * (flat // NZ) + line + lane_id // NZ
        present = x_in & (y_id >= 0) & (y_id < n_ty * (flat // NZ))
        made = coefficients(medium[0, :, part(k)], medium[1, :, part(k)])
        coefs[0, :, part(k)] = jnp.where(present, made[0], 0.0)
        for i in range(1, 4):
            coefs[i, :, part(k)] = made[i]
        coefs[4, :, part(k)] = jnp.where(present, time_step, 0.0)

    def wide_step(n, carry):
        depth_first, depth_last = depth == 0, depth == NZ - 1
        start = jnp.where(n == 0, 1.0, 0.0)

        @pl.when(n == STEPS - 1)
        def _():
            for k in range(chunks):
                value = jnp.zeros((rows, LANES), jnp.float32)
                for i in range(1, STEPS - 1):
                    for c in range(3):
                        value = value + duals[STEPS - 1 - i, c, :, part(k)] * moves[i, c, :, part(k)]
                partial[:, part(k)] = value

        each_trace(n, lambda copy: copy.wait_recv())

        def get(r, c):
            return [wide[r, c, :, part(k)] for k in range(wide_chunks)]

        def pair(up, down, r):
            up = up if r == 0 else roll(up, 4, 0)
            down = roll(down, 4, 0) if r == 0 else down
            return jnp.where(row_id[0:8] < 4, up, down)

        def tall(v):
            return jnp.concatenate([jnp.zeros((rows, LANES), jnp.float32), v], axis=0)

        def x_ahead(k, i):
            tile = (
                recv_a.at[n, 3 * (k // 2)]
                if k < chunks
                else (recv_ahead_up.at[n, 0] if k < chunks + 2 else recv_back_up.at[n, 3])
            )
            i = i + 4 * (k % 2)
            return keep_x_next * tile[i : i + 1]

        def x_back(k, i):
            tile = (
                recv_b.at[n, 3 * (k // 2)]
                if k < chunks
                else (recv_ahead_down.at[n, 1] if k < chunks + 2 else recv_back_down.at[n, 1])
            )
            i = i + 4 * (k % 2)
            return keep_x_prev * tile[i : i + 1]

        def x_corner(k, i):
            tile = recv_c.at[n, k] if k < chunks + 2 else recv_d.at[n, 3 + wide_chunks - k]
            return tile[i : i + 1]

        def at_row(i, v):
            return jnp.where(row_id == i, v, 0.0)

        def y_up(vs, inner_edge, outer_edge):
            turned = [roll(v, NZ, 1) for v in vs]
            out = []
            for k in range(wide_chunks):
                other = turned[(k + 1) % wide_chunks]
                if k == chunks - 1:
                    other = other + inner_edge
                if k == chunks + chunks // 2 - 1:
                    other = jnp.zeros_like(other)
                if k == wide_chunks - 1:
                    other = other + outer_edge
                out.append(jnp.where(low, turned[k], other))
            return out

        def y_down(vs, inner_edge, outer_edge, far):
            turned = [roll(v, NZ, 1) for v in vs]
            out = []
            for k in range(wide_chunks):
                other = turned[(k - 1) % wide_chunks]
                if k == 0:
                    other = other + inner_edge
                if k == chunks:
                    other = other + outer_edge
                if k == chunks + chunks // 2:
                    other = far
                out.append(jnp.where(low, other, turned[k]))
            return out

        zero = jnp.zeros((wide_rows, LANES), jnp.float32)
        for r in range(2):
            def x_up(v, k, c):
                out = roll(v, -1, 0) + at_row(rows - 1, x_ahead(k, 2 * r + c))
                if k >= chunks:
                    out = out + at_row(wide_rows - 1, x_corner(k, 2 * r + c))
                return out

            def x_down(v, k, c, far):
                out = jnp.where(row_id == rows + REACH, far, roll(v, 1, 0))
                out = out + at_row(0, x_back(k, 2 * r + c))
                if k >= chunks:
                    out = out + at_row(rows, x_corner(k, 4 + 2 * r + c))
                return out

            ex, ey, ez = get(r, 0), get(r, 1), get(r, 2)
            got = keep_y_next * jnp.concatenate(
                [
                    recv_c[n, 2 * r],
                    recv_c[n, 2 * r + 1],
                    pair(recv_ahead_up[n, 1], recv_ahead_down[n, 2], r),
                ],
                axis=0,
            )
            corner = tall(pair(recv_a[n, 1], recv_b[n, 1], r))
            y_ez = y_up(ez, got, corner)
            y_ex = y_up(ex, roll(got, NZ, 1), roll(corner, NZ, 1))
            for k in range(wide_chunks):
                x_ez, x_ey = x_up(ez[k], k, 1), x_up(ey[k], k, 0)
                z_ey = jnp.where(depth_last, 0.0, roll(ey[k], -1, 1))
                z_ex = jnp.where(depth_last, 0.0, roll(ex[k], -1, 1))
                curls = (
                    (y_ez[k] - ez[k]) - (z_ey - ey[k]),
                    (z_ex - ex[k]) - (x_ez - ez[k]),
                    (x_ey - ey[k]) - (y_ex[k] - ex[k]),
                )
                for c in range(3):
                    wide[r, 3 + c, :, part(k)] = wide[r, 3 + c, :, part(k)] - coefs[4, :, part(k)] * curls[c]

            hx, hy, hz = get(r, 3), get(r, 4), get(r, 5)
            got = keep_y_prev * jnp.concatenate(
                [
                    recv_d[n, 2 * r],
                    recv_d[n, 2 * r + 1],
                    pair(recv_back_up[n, 2], recv_back_down[n, 0], r),
                ],
                axis=0,
            )
            corner = tall(pair(recv_a[n, 2], recv_b[n, 2], r))
            far_line = at_row(
                rows - 1, (-time_step * start * keep_x_next) * roll(recv_back_up[0, 0, 4 + 2 * r : 5 + 2 * r], NZ, 1)
            )
            far_row = jnp.where(
                low[0:1], 0.0, (time_step * start * keep_y_next) * roll(recv_ahead_down[0, 0, 4 * r + 3 : 4 * r + 4], NZ, 1)
            )
            y_hx = y_down(hx, got, corner, zero)
            y_hz = y_down(hz, roll(got, NZ, 1), roll(corner, NZ, 1), far_line)
            amount = waveforms[0, r, n]
            def electric(k):
                x_hz = x_down(hz[k], k, 1, far_row if k == chunks - 1 else 0.0)
                x_hy = x_down(hy[k], k, 0, 0.0)
                z_hy = jnp.where(depth_first, 0.0, roll(hy[k], 1, 1))
                z_hx = jnp.where(depth_first, 0.0, roll(hx[k], 1, 1))
                curls = (
                    (hz[k] - y_hz[k]) - (hy[k] - z_hy),
                    (hx[k] - z_hx) - (hz[k] - x_hz),
                    (hy[k] - x_hy) - (hx[k] - y_hx[k]),
                )
                for c in range(3):
                    e = wide[r, c, :, part(k)]
                    p = wide[r, 6 + c, :, part(k)]
                    j = wide[r, 9 + c, :, part(k)]
                    j = coefs[1, :, part(k)] * j + coefs[3, :, part(k)] * e - coefs[2, :, part(k)] * p
                    wide[r, 9 + c, :, part(k)] = j
                    wide[r, 6 + c, :, part(k)] = p + time_step * j
                    new = e + coefs[0, :, part(k)] * (curls[c] - j)
                    if k < chunks:
                        new = new - amount * source[r, c, :, part(k)]
                        if r == 0:
                            moves[n, c, :, part(k)] = new[0:rows] - e[0:rows]
                        else:
                            duals[n, c, :, part(k)] = new[0:rows]
                    wide[r, c, :, part(k)] = new
            for k in range(chunks):
                electric(k)

            @pl.when(n < STEPS - 1)
            def _():
                for k in range(chunks, wide_chunks):
                    electric(k)

        return carry

    lax.fori_loop(0, STEPS, wide_step, 0)

    store = pltpu.make_async_copy(wide.at[:, 0:3, 0:rows, 0:flat], final_out.at[0], store_sem.at[0])
    store.start()

    half = rows // 2
    mine = pl.ds(pl.multiple_of(core * half, half), half)
    other = pl.ds(pl.multiple_of((1 - core) * half, half), half)
    pieces = [slice(0, flat // 2), slice(flat // 2, flat)]

    def wave_copies(i, src, dst, target):
        return [
            remote(src(piece), dst(piece), (wave_send_sem.at[i, j], wave_recv_sem.at[i, j]), {"wave": target})
            for j, piece in enumerate(pieces)
        ]

    swap = wave_copies(0, lambda p: partial.at[other, p], lambda p: core_in.at[:, p], wave_core)
    cross = wave_copies(1, lambda p: half_sum.at[:, p], lambda p: chip_in.at[:, p], wave_chip)
    back = wave_copies(2, lambda p: grad_out.at[mine, p], lambda p: grad_out.at[mine, p], wave_core)
    for j in range(2):
        for k in range(j * chunks // 2, (j + 1) * chunks // 2):
            value = partial[:, part(k)]
            for i in (0, STEPS - 1):
                for c in range(3):
                    value = value + duals[STEPS - 1 - i, c, :, part(k)] * moves[i, c, :, part(k)]
            partial[:, part(k)] = value
        swap[j].start()
    for j, p in enumerate(pieces):
        swap[j].wait_recv()
        half_sum[:, p] = partial[mine, p] + core_in[:, p]
        cross[j].start()
    for j, p in enumerate(pieces):
        cross[j].wait_recv()
        grad_out[mine, p] = (contrast * inside[mine, p]) * (half_sum[:, p] + chip_in[:, p])
        back[j].start()
    for j in range(2):
        back[j].wait_recv()
    for copy in swap + cross + back:
        copy.wait_send()

    for copy in medium_copies() + shared_copies(core):
        copy.wait_send()

    def drain(n, carry):
        each_trace(n, lambda copy: copy.wait_send())
        return carry

    lax.fori_loop(0, STEPS, drain, 0)
    store.wait()


def put_out(grad, final, grad_out, final_out, sem):
    copies = (
        pltpu.make_async_copy(final, final_out, sem.at[0]),
        pltpu.make_async_copy(grad, grad_out, sem.at[1]),
    )
    for copy in copies:
        copy.start()
    for copy in copies:
        copy.wait()


def solution(mesh):
    n_wave, n_tx, n_ty = mesh.shape["wave"], mesh.shape["tx"], mesh.shape["ty"]

    def on_device(fields, profiles, waveforms, material_map, density, table, planes, box):
        rows, flat = material_map.shape
        f32 = jnp.float32
        vmem, smem, anywhere = pltpu.VMEM, pltpu.SMEM, pl.ANY
        spaces = (anywhere,) * 8
        wide_rows, wide_flat = rows + 2 * REACH, flat + 2 * REACH * NZ
        grad, final = pl.pallas_call(
            functools.partial(kernel, (n_wave, n_tx, n_ty, rows, flat)),
            out_shape=(vmem((rows, flat), f32), vmem((1, 2, 3, rows, flat), f32)),
            in_specs=[pl.BlockSpec(memory_space=space) for space in spaces],
            out_specs=(pl.BlockSpec(memory_space=vmem),) * 2,
            scratch_shapes=[
                vmem((2, 12, rows, flat), f32),
                vmem((2, 12, wide_rows, wide_flat), f32),
                vmem((3, 2, flat), f32),
                vmem((2, 3, wide_rows, flat), f32),
                vmem((2, wide_rows, wide_flat), f32),
                vmem((5, wide_rows, wide_flat), f32),
                vmem((rows, flat), f32),
                vmem((STEPS, 3, rows, flat), f32),
                vmem((STEPS, 3, rows, flat), f32),
                *(vmem((STEPS, tiles, 8, LANES), f32) for tiles in (4, 5, 6, 6)),
                *(vmem((STEPS, tiles, 8, LANES), f32) for tiles in (4, 4, 6, 6, 2, 3, 4, 2)),
                smem(waveforms.shape, f32),
                vmem((rows, flat), jnp.int32),
                vmem((rows, flat), f32),
                smem(table.shape, f32),
                smem(planes.shape, jnp.int32),
                smem(box.shape, jnp.int32),
                vmem((rows, flat), f32),
                vmem((rows // 2, flat), f32),
                vmem((rows // 2, flat), f32),
                vmem((rows // 2, flat), f32),
                pltpu.SemaphoreType.DMA((STEPS, FLOWS)),
                pltpu.SemaphoreType.DMA((STEPS, FLOWS)),
                pltpu.SemaphoreType.DMA((10,)),
                pltpu.SemaphoreType.DMA((10,)),
                pltpu.SemaphoreType.DMA((3, 2)),
                pltpu.SemaphoreType.DMA((3, 2)),
                pltpu.SemaphoreType.DMA((10,)),
                pltpu.SemaphoreType.DMA((2,)),
            ],
            compiler_params=pltpu.CompilerParams(collective_id=0, has_side_effects=True),
        )(fields, jnp.transpose(profiles, (0, 2, 1, 3)), waveforms, material_map, density, table, planes, box)
        return pl.pallas_call(
            put_out,
            out_shape=(
                jax.ShapeDtypeStruct((rows, flat), f32),
                jax.ShapeDtypeStruct((1, 2, 3, rows, flat), f32),
            ),
            in_specs=[pl.BlockSpec(memory_space=vmem)] * 2,
            out_specs=(pl.BlockSpec(memory_space=anywhere),) * 2,
            scratch_shapes=[pltpu.SemaphoreType.DMA((2,))],
            compiler_params=pltpu.CompilerParams(vmem_limit_bytes=1 << 20),
        )(grad, final)

    placed = (
        P("wave", None, None, "tx", "ty"),
        P("wave", None, None, None),
        P("wave", None, None),
        P("tx", "ty"),
        P("tx", "ty"),
        P(),
        P(),
        P(),
    )
    return jax.shard_map(
        on_device,
        mesh=mesh,
        in_specs=placed,
        out_specs=(P("tx", "ty"), P("wave", None, None, "tx", "ty")),
        check_vma=False,
    )
```

```python
import functools

import jax
import jax.numpy as jnp
from jax import lax
from jax.experimental import pallas as pl
from jax.experimental.pallas import tpu as pltpu
from jax.sharding import PartitionSpec as P

NZ = 64
STEPS = 5
NMAT = 3
LANES = 128
REACH = 4
FLOWS = 8
MESH = pl.DeviceIdType.MESH

time_step = 0.5
contrast = 2.0


def kernel(
    sizes,
    fields,
    profiles,
    waveforms_in,
    material_in,
    density_in,
    table_in,
    planes_in,
    box_in,
    grad_out,
    final_out,
    alone,
    wide,
    profile,
    source,
    medium,
    coefs,
    inside,
    moves,
    duals,
    send_a,
    send_b,
    send_c,
    send_d,
    recv_a,
    recv_b,
    recv_c,
    recv_d,
    recv_ahead_up,
    recv_ahead_down,
    recv_back_up,
    recv_back_down,
    waveforms,
    material_map,
    density,
    table,
    planes,
    box,
    partial,
    core_in,
    half_sum,
    chip_in,
    send_sem,
    recv_sem,
    once_send_sem,
    once_recv_sem,
    wave_send_sem,
    wave_recv_sem,
    load_sem,
    store_sem,
    answer,
):
    n_wave, n_tx, n_ty, rows, flat = sizes
    chunks = flat // LANES
    wide_chunks = 2 * chunks
    wide_rows = rows + 2 * REACH
    edge = REACH * NZ
    wave = lax.axis_index("wave")
    tx = lax.axis_index("tx")
    ty = lax.axis_index("ty")
    tx_next, tx_prev = lax.rem(tx + 1, n_tx), lax.rem(tx + n_tx - 1, n_tx)
    ty_next, ty_prev = lax.rem(ty + 1, n_ty), lax.rem(ty + n_ty - 1, n_ty)
    core = lax.rem(wave, 2)
    wave_core = wave + 1 - 2 * core
    wave_chip = lax.rem(wave + 2, n_wave)

    load = pltpu.make_async_copy(fields.at[0, :, 0:6], alone.at[:, 0:6], load_sem.at[0])
    load.start()
    load_rest = pltpu.make_async_copy(fields.at[0, :, 6:12], alone.at[:, 6:12], load_sem.at[3])
    load_rest.start()
    load_profile = pltpu.make_async_copy(
        profiles.at[0, :, :, pl.ds(pl.multiple_of(ty * flat, LANES), flat)], profile, load_sem.at[1]
    )
    load_profile.start()
    small = [
        pltpu.make_async_copy(src, dst, load_sem.at[4 + i])
        for i, (src, dst) in enumerate(
            (
                (material_in, material_map),
                (density_in, density),
                (table_in, table),
                (box_in, box),
                (planes_in, planes),
                (waveforms_in, waveforms),
            )
        )
    ]
    for copy in small:
        copy.start()
    load_wide = pltpu.make_async_copy(fields.at[0], wide.at[:, :, 0:rows, 0:flat], load_sem.at[2])

    barrier = pltpu.get_barrier_semaphore()
    low_low = {"tx": tx_prev, "ty": ty_prev}
    low_high = {"tx": tx_prev, "ty": ty_next}
    high_low = {"tx": tx_next, "ty": ty_prev}
    high_high = {"tx": tx_next, "ty": ty_next}
    far_half = wave // 2
    more_x, less_x = tx < n_tx - 1, tx > 0
    more_y, less_y = ty < n_ty - 1, ty > 0
    around = {
        "y_prev": ({"ty": ty_prev}, less_y, more_y),
        "y_next": ({"ty": ty_next}, more_y, less_y),
        "x_prev": ({"tx": tx_prev}, less_x, more_x),
        "x_next": ({"tx": tx_next}, more_x, less_x),
        "low_low": (low_low, less_x & less_y, more_x & more_y),
        "low_high": (low_high, less_x & more_y, more_x & less_y),
        "high_low": (high_low, more_x & less_y, less_x & more_y),
        "high_high": (high_high, more_x & more_y, less_x & less_y),
    }

    def clear(ref):
        ref[...] = jnp.zeros(ref.shape, jnp.float32)

    clear(recv_c.at[2:STEPS, 5])
    clear(recv_d.at[2:STEPS, 5])
    clear(recv_ahead_up.at[STEPS - 1])
    clear(recv_back_down.at[STEPS - 1])
    for name, ref in (
        ("y_prev", recv_c),
        ("y_next", recv_d),
        ("x_prev", recv_a),
        ("x_next", recv_b),
        ("low_low", recv_ahead_up),
        ("low_high", recv_back_up),
        ("high_low", recv_ahead_down),
        ("high_high", recv_back_down),
    ):

        @pl.when(jnp.logical_not(around[name][2]))
        def _(ref=ref):
            clear(ref)

    @pl.when(jnp.logical_not(more_x & less_x & more_y & less_y))
    def _():
        clear(medium.at[:, rows:wide_rows])
        clear(medium.at[:, 0:rows, flat : 2 * flat])

    @pl.when(far_half == 0)
    def _():
        pl.semaphore_signal(barrier, inc=1, device_id={"wave": wave_chip}, device_id_type=MESH)

    pl.semaphore_signal(barrier, inc=1, device_id={"wave": wave_core}, device_id_type=MESH)
    greetings = far_half + 1
    for target, there, _ in around.values():
        greetings = greetings + jnp.where(there, 1, 0)

        @pl.when(there)
        def _(target=target):
            pl.semaphore_signal(barrier, inc=1, device_id=target, device_id_type=MESH)

    def ids(count):
        row = lax.broadcasted_iota(jnp.int32, (count, LANES), 0)
        lane = lax.broadcasted_iota(jnp.int32, (count, LANES), 1)
        return row, lane, lane < NZ, lax.rem(lane, NZ)

    def part(k):
        return slice(k * LANES, (k + 1) * LANES)

    def per_material(material, values):
        out = jnp.where(material == 0, values[0], values[1])
        for m in range(2, NMAT):
            out = jnp.where(material == m, values[m], out)
        return out

    row_id, lane_id, low, depth = ids(rows)

    def coefficients(reach, material):
        omega = per_material(material, [table[m, 2] for m in range(NMAT)])
        spread = per_material(material, [table[m, 1] for m in range(NMAT)])
        damping = per_material(material, [table[m, 3] for m in range(NMAT)])
        denom = 1.0 + 0.25 * damping
        drive = omega * omega * time_step / denom
        return reach, (1.0 - 0.25 * damping) / denom, drive, drive * spread

    def make_medium():
        for copy in small[:4]:
            copy.wait()
        for k in range(chunks):
            material = material_map[:, part(k)]
            eps = per_material(material, [table[m, 0] for m in range(NMAT)])
            x_id = row_id + tx * rows
            y_id = ty * (flat // NZ) + 2 * k + lane_id // NZ
            in_box = (
                (x_id >= box[0])
                & (x_id < box[1])
                & (y_id >= box[2])
                & (y_id < box[3])
                & (depth >= box[4])
                & (depth < box[5])
            )
            within = jnp.where(in_box, 1.0, 0.0)
            inside[:, part(k)] = within
            medium[0, 0:rows, part(k)] = time_step / (eps + (within * density[:, part(k)]) * contrast)
            medium[1, 0:rows, part(k)] = material.astype(jnp.float32)

    def prepare():
        for copy in small[4:]:
            copy.wait()
        load_wide.start()
        load_rest.wait()
        load_profile.wait()
        for k in range(chunks):
            made = coefficients(medium[0, 0:rows, part(k)], material_map[:, part(k)])
            for i in range(4):
                coefs[i, 0:rows, part(k)] = made[i]

        for r in range(2):
            on_plane = jnp.where(row_id + tx * rows == planes[r], 1.0, 0.0)
            for c in range(3):
                for k in range(chunks):
                    source[r, c, 0:rows, part(k)] = (
                        coefs[0, 0:rows, part(k)] * on_plane * profile[c, r : r + 1, part(k)]
                    )
                    source[r, c, rows:wide_rows, part(k)] = jnp.zeros((2 * REACH, LANES), jnp.float32)

    def roll(v, shift, axis):
        return pltpu.roll(v, shift % v.shape[axis], axis)

    def remote(src, dst, sems, target):
        return pltpu.make_async_remote_copy(
            src_ref=src,
            dst_ref=dst,
            send_sem=sems[0],
            recv_sem=sems[1],
            device_id=target,
            device_id_type=MESH,
        )

    top, bottom = slice(0, REACH), slice(rows - REACH, rows)
    after, before = slice(rows, rows + REACH), slice(rows + REACH, wide_rows)
    left, right = slice(0, edge), slice(flat - edge, flat)
    beyond, ahead_of = slice(flat, flat + edge), slice(flat + edge, flat + 2 * edge)
    whole, inner = slice(0, rows), slice(0, flat)

    def guarded(act, ways, sending):
        for name, active, copy in ways:
            when = around[name][1 if sending else 2]
            if active is not None:
                when = when & active

            @pl.when(when)
            def _(copy=copy):
                act(copy)

    def medium_copies():
        ways = (
            ("y_prev", whole, left, whole, beyond),
            ("y_next", whole, right, whole, ahead_of),
            ("low_low", top, left, after, beyond),
            ("low_high", top, right, after, ahead_of),
            ("high_low", bottom, left, before, beyond),
            ("high_high", bottom, right, before, ahead_of),
            ("x_prev", top, inner, after, inner),
            ("x_next", bottom, inner, before, inner),
        )
        return [
            (
                name,
                None,
                remote(
                    medium.at[core, a, b],
                    medium.at[core, c, d],
                    (once_send_sem.at[i], once_recv_sem.at[i]),
                    around[name][0],
                ),
            )
            for i, (name, a, b, c, d) in enumerate(ways)
        ]

    def shared_copies(plane):
        areas = ((slice(0, rows), slice(flat, 2 * flat)), (slice(rows, wide_rows), slice(0, 2 * flat)))
        return [
            remote(
                medium.at[plane, a, b],
                medium.at[plane, a, b],
                (once_send_sem.at[8 + i], once_recv_sem.at[8 + i]),
                {"wave": wave_core},
            )
            for i, (a, b) in enumerate(areas)
        ]

    def trace_copies(n):
        first, later, early, late, before_last = n == 0, n > 0, n < 2, n >= 2, n < STEPS - 1
        ways = (
            ("y_prev", early, 0, send_c.at[n, 0:6], recv_c.at[n, 0:6]),
            ("y_prev", late, 0, send_c.at[n, 0:5], recv_c.at[n, 0:5]),
            ("y_next", early, 1, send_d.at[n, 0:6], recv_d.at[n, 0:6]),
            ("y_next", late, 1, send_d.at[n, 0:5], recv_d.at[n, 0:5]),
            ("low_high", first, 2, send_a.at[n], recv_back_up.at[n]),
            ("low_high", later, 2, send_a.at[n, 2:4], recv_back_up.at[n, 2:4]),
            ("high_low", first, 3, send_b.at[n, 0:3], recv_ahead_down.at[n]),
            ("high_low", later, 3, send_b.at[n, 1:3], recv_ahead_down.at[n, 1:3]),
            ("low_low", before_last, 4, send_a.at[n, 0:2], recv_ahead_up.at[n]),
            ("high_high", before_last, 5, send_b.at[n, 3:5], recv_back_down.at[n]),
            ("x_prev", None, 6, send_a.at[n], recv_a.at[n]),
            ("x_next", None, 7, send_b.at[n, 1:5], recv_b.at[n]),
        )
        return [
            (name, active, remote(src, dst, (send_sem.at[n, i], recv_sem.at[n, i]), around[name][0]))
            for name, active, i, src, dst in ways
        ]

    make_medium()
    pl.semaphore_wait(barrier, greetings)

    @pl.when(far_half == 1)
    def _():
        pl.semaphore_signal(answer, inc=1, device_id={"wave": wave_chip}, device_id_type=MESH)

    guarded(lambda copy: copy.start(), medium_copies(), True)
    load.wait()

    def alone_step(n, carry):
        depth_first, depth_last = depth == 0, depth == NZ - 1
        first_row, last_row = row_id == 0, row_id == rows - 1

        def y_up(vs):
            turned = [roll(v, NZ, 1) for v in vs] + [jnp.zeros((rows, LANES), jnp.float32)]
            return [jnp.where(low, turned[k], turned[k + 1]) for k in range(chunks)]

        def y_down(vs):
            turned = [jnp.zeros((rows, LANES), jnp.float32)] + [roll(v, NZ, 1) for v in vs]
            return [jnp.where(low, turned[k], turned[k + 1]) for k in range(chunks)]

        def get(r, c):
            return [alone[r, c, :, part(k)] for k in range(chunks)]

        for r in range(2):
            ex, ey, ez = get(r, 0), get(r, 1), get(r, 2)
            y_ez, y_ex = y_up(ez), y_up(ex)
            for k in range(chunks):
                x_ez = jnp.where(last_row, 0.0, roll(ez[k], -1, 0))
                x_ey = jnp.where(last_row, 0.0, roll(ey[k], -1, 0))
                z_ey = jnp.where(depth_last, 0.0, roll(ey[k], -1, 1))
                z_ex = jnp.where(depth_last, 0.0, roll(ex[k], -1, 1))
                curl_x = (y_ez[k] - ez[k]) - (z_ey - ey[k])
                curl_y = (z_ex - ex[k]) - (x_ez - ez[k])
                curl_z = (x_ey - ey[k]) - (y_ex[k] - ex[k])
                hx = alone[r, 3, :, part(k)] - time_step * curl_x
                hy = alone[r, 4, :, part(k)] - time_step * curl_y
                hz = alone[r, 5, :, part(k)] - time_step * curl_z
                alone[r, 3, :, part(k)] = hx
                alone[r, 4, :, part(k)] = hy
                alone[r, 5, :, part(k)] = hz
                e_edge = (ey[k][0:1], ez[k][0:1])
                h_edge = (hy[rows - 1 : rows], hz[rows - 1 : rows])
                side, tile, beside = (
                    (send_c, 4 + k, 0) if k < chunks // 2 else (send_d, 3 + chunks - k, 3)
                )
                for c in range(2):
                    i, j = 4 * (k % 2) + 2 * r + c, 2 * r + c
                    send_a[n, beside, i : i + 1] = e_edge[c]
                    send_b[n, beside + 1, i : i + 1] = h_edge[c]
                    side[n, tile, j : j + 1] = e_edge[c]
                    side[n, tile, 4 + j : 5 + j] = h_edge[c]
                spot = slice(4 * r, 4 * r + 4)
                if k == 0:
                    line = jnp.where(low, ex[k], roll(ez[k], NZ, 1))
                    upper, lower = line[0:8], line[8:16]
                    send_c[n, 2 * r], send_c[n, 2 * r + 1] = upper, lower
                    send_a[n, 1, spot] = (upper if r == 0 else roll(upper, 4, 0))[spot]
                    send_b[n, 2, spot] = (roll(lower, 4, 0) if r == 0 else lower)[spot]
                    send_b[n, 0, spot] = (lower if r == 0 else roll(lower, 4, 0))[spot]
                if k == chunks - 1:
                    line = jnp.where(low, roll(hx, NZ, 1), hz)
                    upper, lower = line[0:8], line[8:16]
                    send_d[n, 2 * r], send_d[n, 2 * r + 1] = upper, lower
                    send_a[n, 2, spot] = (upper if r == 0 else roll(upper, 4, 0))[spot]
                    send_b[n, 3, spot] = (roll(lower, 4, 0) if r == 0 else lower)[spot]

        guarded(lambda copy: copy.start(), trace_copies(n), True)

        @pl.when(n == 0)
        def _():
            prepare()

        @pl.when(n < STEPS - 1)
        def _():
            for r in range(2):
                hx, hy, hz = get(r, 3), get(r, 4), get(r, 5)
                y_hz, y_hx = y_down(hz), y_down(hx)
                amount = waveforms[0, r, n]
                for k in range(chunks):
                    x_hz = jnp.where(first_row, 0.0, roll(hz[k], 1, 0))
                    x_hy = jnp.where(first_row, 0.0, roll(hy[k], 1, 0))
                    z_hy = jnp.where(depth_first, 0.0, roll(hy[k], 1, 1))
                    z_hx = jnp.where(depth_first, 0.0, roll(hx[k], 1, 1))
                    curls = (
                        (hz[k] - y_hz[k]) - (hy[k] - z_hy),
                        (hx[k] - z_hx) - (hz[k] - x_hz),
                        (hy[k] - x_hy) - (hx[k] - y_hx[k]),
                    )
                    for c in range(3):
                        e = alone[r, c, :, part(k)]
                        p = alone[r, 6 + c, :, part(k)]
                        j = alone[r, 9 + c, :, part(k)]
                        j = (
                            coefs[1, 0:rows, part(k)] * j
                            + coefs[3, 0:rows, part(k)] * e
                            - coefs[2, 0:rows, part(k)] * p
                        )
                        alone[r, 9 + c, :, part(k)] = j
                        alone[r, 6 + c, :, part(k)] = p + time_step * j
                        alone[r, c, :, part(k)] = (
                            e
                            + coefs[0, 0:rows, part(k)] * (curls[c] - j)
                            - amount * source[r, c, 0:rows, part(k)]
                        )

        return carry

    lax.fori_loop(0, STEPS, alone_step, 0)

    guarded(lambda copy: copy.wait_recv(), medium_copies(), False)
    for copy in shared_copies(core):
        copy.start()

    load_wide.wait()
    for r in range(2):
        for c in range(12):
            for k in range(wide_chunks):
                if k < chunks:
                    wide[r, c, rows:wide_rows, part(k)] = jnp.zeros((2 * REACH, LANES), jnp.float32)
                else:
                    wide[r, c, :, part(k)] = jnp.zeros((wide_rows, LANES), jnp.float32)

    for copy in shared_copies(1 - core):
        copy.wait_recv()
    row_id, lane_id, low, depth = ids(wide_rows)
    near_row = jnp.where(row_id < rows + REACH, row_id, row_id - wide_rows)
    x_in = (near_row + tx * rows >= 0) & (near_row + tx * rows < n_tx * rows)
    for k in range(wide_chunks):
        line = 2 * k if k < chunks + chunks // 2 else 2 * (k - wide_chunks)
        y_id = ty * (flat // NZ) + line + lane_id // NZ
        present = x_in & (y_id >= 0) & (y_id < n_ty * (flat // NZ))
        made = coefficients(medium[0, :, part(k)], medium[1, :, part(k)])
        coefs[0, :, part(k)] = jnp.where(present, made[0], 0.0)
        for i in range(1, 4):
            coefs[i, :, part(k)] = made[i]
        coefs[4, :, part(k)] = jnp.where(present, time_step, 0.0)

    def wide_step(n, carry):
        depth_first, depth_last = depth == 0, depth == NZ - 1
        start = jnp.where(n == 0, 1.0, 0.0)

        @pl.when(n == STEPS - 1)
        def _():
            for k in range(chunks):
                value = jnp.zeros((rows, LANES), jnp.float32)
                for i in range(1, STEPS - 1):
                    for c in range(3):
                        value = value + duals[STEPS - 1 - i, c, :, part(k)] * moves[i, c, :, part(k)]
                partial[:, part(k)] = value

        guarded(lambda copy: copy.wait_recv(), trace_copies(n), False)

        def pair(up, down, r):
            up = up if r == 0 else roll(up, 4, 0)
            down = roll(down, 4, 0) if r == 0 else down
            return jnp.where(row_id[0:8] < 4, up, down)

        def tall(v):
            return jnp.concatenate([jnp.zeros((rows, LANES), jnp.float32), v], axis=0)

        def x_ahead(k, i):
            tile = (
                recv_a.at[n, 3 * (k // 2)]
                if k < chunks
                else (recv_ahead_up.at[n, 0] if k < chunks + 2 else recv_back_up.at[n, 3])
            )
            i = i + 4 * (k % 2)
            return tile[i : i + 1]

        def x_back(k, i):
            tile = (
                recv_b.at[n, 3 * (k // 2)]
                if k < chunks
                else (recv_ahead_down.at[n, 1] if k < chunks + 2 else recv_back_down.at[n, 1])
            )
            i = i + 4 * (k % 2)
            return tile[i : i + 1]

        def x_corner(k, i):
            tile = recv_c.at[n, k] if k < chunks + 2 else recv_d.at[n, 3 + wide_chunks - k]
            return tile[i : i + 1]

        def edit(v, i, change):
            groups = [v[8 * g : 8 * g + 8] for g in range(wide_rows // 8)]
            g = i // 8
            groups[g] = jnp.where(row_id[0:8] == i % 8, change(groups[g]), groups[g])
            return jnp.concatenate(groups, axis=0)

        class Turned:
            def __init__(self, r, c):
                self.r, self.c, self.held = r, c, {}

            def __getitem__(self, k):
                k = k % wide_chunks
                if k not in self.held:
                    self.held[k] = roll(wide[self.r, self.c, :, part(k)], NZ, 1)
                return self.held[k]

        def y_up(turned, k, inner_edge, outer_edge):
            if k == chunks + chunks // 2 - 1:
                return jnp.where(low, turned[k], 0.0)
            other = turned[k + 1]
            if k == chunks - 1:
                other = other + inner_edge
            if k == wide_chunks - 1:
                other = other + outer_edge
            return jnp.where(low, turned[k], other)

        def y_down(turned, k, inner_edge, outer_edge, far):
            if k == chunks + chunks // 2:
                return jnp.where(low, far, turned[k])
            other = turned[k - 1]
            if k == 0:
                other = other + inner_edge
            if k == chunks:
                other = other + outer_edge
            return jnp.where(low, other, turned[k])

        def x_up(v, k, i):
            out = edit(roll(v, -1, 0), rows - 1, lambda g: g + x_ahead(k, i))
            if k >= chunks:
                out = edit(out, wide_rows - 1, lambda g: g + x_corner(k, i))
            return out

        def x_down(v, k, i, far):
            out = edit(roll(v, 1, 0), rows + REACH, lambda g: far)
            out = edit(out, 0, lambda g: g + x_back(k, i))
            if k >= chunks:
                out = edit(out, rows, lambda g: g + x_corner(k, 4 + i))
            return out

        for r in range(2):
            got = jnp.concatenate(
                [
                    recv_c[n, 2 * r],
                    recv_c[n, 2 * r + 1],
                    pair(recv_ahead_up[n, 1], recv_ahead_down[n, 2], r),
                ],
                axis=0,
            )
            corner = tall(pair(recv_a[n, 1], recv_b[n, 1], r))

            def magnetic(ks):
                turned_z, turned_x = Turned(r, 2), Turned(r, 0)
                for k in ks:
                    ex, ey, ez = (wide[r, c, :, part(k)] for c in range(3))
                    y_ez = y_up(turned_z, k, got, corner)
                    y_ex = y_up(turned_x, k, roll(got, NZ, 1), roll(corner, NZ, 1))
                    x_ez, x_ey = x_up(ez, k, 2 * r + 1), x_up(ey, k, 2 * r)
                    z_ey = jnp.where(depth_last, 0.0, roll(ey, -1, 1))
                    z_ex = jnp.where(depth_last, 0.0, roll(ex, -1, 1))
                    curls = (
                        (y_ez - ez) - (z_ey - ey),
                        (z_ex - ex) - (x_ez - ez),
                        (x_ey - ey) - (y_ex - ex),
                    )
                    half_step = coefs[4, :, part(k)]
                    for c in range(3):
                        wide[r, 3 + c, :, part(k)] = wide[r, 3 + c, :, part(k)] - half_step * curls[c]

            magnetic((wide_chunks - 1, *range(chunks + 1)))

            @pl.when(n < 3)
            def _():
                magnetic((chunks + 1, chunks + 2))

        for r in range(2):
            got = jnp.concatenate(
                [
                    recv_d[n, 2 * r],
                    recv_d[n, 2 * r + 1],
                    pair(recv_back_up[n, 2], recv_back_down[n, 0], r),
                ],
                axis=0,
            )
            corner = tall(pair(recv_a[n, 2], recv_b[n, 2], r))
            amount = waveforms[0, r, n]

            def electric(ks):
                turned_x, turned_z = Turned(r, 3), Turned(r, 5)
                for k in ks:
                    hx, hy, hz = (wide[r, 3 + c, :, part(k)] for c in range(3))
                    far_line, far_row = 0.0, jnp.zeros((1, LANES), jnp.float32)
                    if k == chunks + chunks // 2:
                        far = roll(recv_back_up[0, 0, 4 + 2 * r : 5 + 2 * r], NZ, 1)
                        far_line = jnp.where(row_id == rows - 1, (-time_step * start) * far, 0.0)
                    if k == chunks - 1:
                        far = roll(recv_ahead_down[0, 0, 4 * r + 3 : 4 * r + 4], NZ, 1)
                        far_row = jnp.where(low[0:1], 0.0, (time_step * start) * far)
                    y_hx = y_down(turned_x, k, got, corner, 0.0)
                    y_hz = y_down(turned_z, k, roll(got, NZ, 1), roll(corner, NZ, 1), far_line)
                    x_hz = x_down(hz, k, 2 * r + 1, far_row)
                    x_hy = x_down(hy, k, 2 * r, jnp.zeros((1, LANES), jnp.float32))
                    z_hy = jnp.where(depth_first, 0.0, roll(hy, 1, 1))
                    z_hx = jnp.where(depth_first, 0.0, roll(hx, 1, 1))
                    curls = (
                        (hz - y_hz) - (hy - z_hy),
                        (hx - z_hx) - (hz - x_hz),
                        (hy - x_hy) - (hx - y_hx),
                    )
                    reach, decay, drive, coupled = (coefs[i, :, part(k)] for i in range(4))
                    for c in range(3):
                        e = wide[r, c, :, part(k)]
                        p = wide[r, 6 + c, :, part(k)]
                        j = wide[r, 9 + c, :, part(k)]
                        j = decay * j + coupled * e - drive * p
                        wide[r, 9 + c, :, part(k)] = j
                        wide[r, 6 + c, :, part(k)] = p + time_step * j
                        new = e + reach * (curls[c] - j)
                        if k < chunks:
                            new = new - amount * source[r, c, :, part(k)]
                            if r == 0:
                                moves[n, c, :, part(k)] = new[0:rows] - e[0:rows]
                            else:
                                duals[n, c, :, part(k)] = new[0:rows]
                        wide[r, c, :, part(k)] = new

            electric(range(chunks))

            @pl.when(n < STEPS - 1)
            def _():
                electric((chunks, wide_chunks - 1))

            @pl.when(n < 2)
            def _():
                electric((chunks + 1, chunks + 2))

        return carry

    lax.fori_loop(0, STEPS, wide_step, 0)

    store = pltpu.make_async_copy(wide.at[:, 0:3, 0:rows, 0:flat], final_out.at[0], store_sem.at[0])
    store.start()

    half = rows // 2
    mine = pl.ds(pl.multiple_of(core * half, half), half)
    other = pl.ds(pl.multiple_of((1 - core) * half, half), half)
    pieces = [slice(0, flat // 2), slice(flat // 2, flat)]

    def wave_copies(i, src, dst, target):
        return [
            remote(src(piece), dst(piece), (wave_send_sem.at[i, j], wave_recv_sem.at[i, j]), {"wave": target})
            for j, piece in enumerate(pieces)
        ]

    swap = wave_copies(0, lambda p: partial.at[other, p], lambda p: core_in.at[:, p], wave_core)
    cross = wave_copies(1, lambda p: half_sum.at[:, p], lambda p: chip_in.at[:, p], wave_chip)
    back = wave_copies(2, lambda p: grad_out.at[mine, p], lambda p: grad_out.at[mine, p], wave_core)
    for j in range(2):
        for k in range(j * chunks // 2, (j + 1) * chunks // 2):
            value = partial[:, part(k)]
            for i in (0, STEPS - 1):
                for c in range(3):
                    value = value + duals[STEPS - 1 - i, c, :, part(k)] * moves[i, c, :, part(k)]
            partial[:, part(k)] = value
        swap[j].start()

    @pl.when(far_half == 0)
    def _():
        pl.semaphore_wait(answer, 1)

    for j, p in enumerate(pieces):
        swap[j].wait_recv()
        half_sum[:, p] = partial[mine, p] + core_in[:, p]
        cross[j].start()
    guarded(lambda copy: copy.wait_send(), medium_copies(), True)
    for copy in shared_copies(core):
        copy.wait_send()

    def drain(n, carry):
        guarded(lambda copy: copy.wait_send(), trace_copies(n), True)
        return carry

    lax.fori_loop(0, STEPS, drain, 0)

    for j, p in enumerate(pieces):
        cross[j].wait_recv()
        grad_out[mine, p] = (contrast * inside[mine, p]) * (half_sum[:, p] + chip_in[:, p])
        back[j].start()
    for j in range(2):
        back[j].wait_recv()
    for copy in swap + cross + back:
        copy.wait_send()

    store.wait()


def put_out(grad, final, grad_out, final_out, sem):
    copies = (
        pltpu.make_async_copy(final, final_out, sem.at[0]),
        pltpu.make_async_copy(grad, grad_out, sem.at[1]),
    )
    for copy in copies:
        copy.start()
    for copy in copies:
        copy.wait()


def solution(mesh):
    n_wave, n_tx, n_ty = mesh.shape["wave"], mesh.shape["tx"], mesh.shape["ty"]

    def on_device(fields, profiles, waveforms, material_map, density, table, planes, box):
        rows, flat = material_map.shape
        f32 = jnp.float32
        vmem, smem, anywhere = pltpu.VMEM, pltpu.SMEM, pl.ANY
        spaces = (anywhere,) * 8
        wide_rows, wide_flat = rows + 2 * REACH, flat + 2 * REACH * NZ
        grad, final = pl.pallas_call(
            functools.partial(kernel, (n_wave, n_tx, n_ty, rows, flat)),
            out_shape=(vmem((rows, flat), f32), vmem((1, 2, 3, rows, flat), f32)),
            in_specs=[pl.BlockSpec(memory_space=space) for space in spaces],
            out_specs=(pl.BlockSpec(memory_space=vmem),) * 2,
            scratch_shapes=[
                vmem((2, 12, rows, flat), f32),
                vmem((2, 12, wide_rows, wide_flat), f32),
                vmem((3, 2, flat), f32),
                vmem((2, 3, wide_rows, flat), f32),
                vmem((2, wide_rows, wide_flat), f32),
                vmem((5, wide_rows, wide_flat), f32),
                vmem((rows, flat), f32),
                vmem((STEPS, 3, rows, flat), f32),
                vmem((STEPS, 3, rows, flat), f32),
                *(vmem((STEPS, tiles, 8, LANES), f32) for tiles in (4, 5, 6, 6)),
                *(vmem((STEPS, tiles, 8, LANES), f32) for tiles in (4, 4, 6, 6, 2, 3, 4, 2)),
                smem(waveforms.shape, f32),
                vmem((rows, flat), jnp.int32),
                vmem((rows, flat), f32),
                smem(table.shape, f32),
                smem(planes.shape, jnp.int32),
                smem(box.shape, jnp.int32),
                vmem((rows, flat), f32),
                vmem((rows // 2, flat), f32),
                vmem((rows // 2, flat), f32),
                vmem((rows // 2, flat), f32),
                pltpu.SemaphoreType.DMA((STEPS, FLOWS)),
                pltpu.SemaphoreType.DMA((STEPS, FLOWS)),
                pltpu.SemaphoreType.DMA((10,)),
                pltpu.SemaphoreType.DMA((10,)),
                pltpu.SemaphoreType.DMA((3, 2)),
                pltpu.SemaphoreType.DMA((3, 2)),
                pltpu.SemaphoreType.DMA((10,)),
                pltpu.SemaphoreType.DMA((2,)),
                pltpu.SemaphoreType.REGULAR,
            ],
            compiler_params=pltpu.CompilerParams(collective_id=0, has_side_effects=True),
        )(fields, jnp.transpose(profiles, (0, 2, 1, 3)), waveforms, material_map, density, table, planes, box)
        return pl.pallas_call(
            put_out,
            out_shape=(
                jax.ShapeDtypeStruct((rows, flat), f32),
                jax.ShapeDtypeStruct((1, 2, 3, rows, flat), f32),
            ),
            in_specs=[pl.BlockSpec(memory_space=vmem)] * 2,
            out_specs=(pl.BlockSpec(memory_space=anywhere),) * 2,
            scratch_shapes=[pltpu.SemaphoreType.DMA((2,))],
            compiler_params=pltpu.CompilerParams(vmem_limit_bytes=1 << 20),
        )(grad, final)

    placed = (
        P("wave", None, None, "tx", "ty"),
        P("wave", None, None, None),
        P("wave", None, None),
        P("tx", "ty"),
        P("tx", "ty"),
        P(),
        P(),
        P(),
    )
    return jax.shard_map(
        on_device,
        mesh=mesh,
        in_specs=placed,
        out_specs=(P("tx", "ty"), P("wave", None, None, "tx", "ty")),
        check_vma=False,
    )
```
